256 devices in a mesh: row: 32 (over x, z), col: 8 (over y, core).
Axes of the slice: x: 4, y: 4, z: 8, core: 2. Of those that a mesh axis runs over, the one named last changes fastest.
Arguments:
- front_tiles: bfloat16 [4, 8192, 2, 2048], P(None, 'row', None, 'col'), may hold values from -6 to 6
- fill_pattern: int32 [4, 32, 2, 8], P(None, 'row', None, 'col'), may hold values from 0 to 1, as said below
- w_inverse: bfloat16 [2, 256, 256], replicated, may hold values from -0.015625 to 0.015625
- samples: bfloat16 [4, 8192, 512], P(None, 'row'), may hold values from -6 to 6
Outputs:
- factor_slab: bfloat16 [4, 8192, 2, 2048], P(None, 'row', None, 'col')
- solved_rows: bfloat16 [4, 8192, 512], P(None, 'row')
The draws below stay inside these ranges and needn't reach their ends.
Inputs may be any that keep to these rules, and one draw needn't show every extreme that they name: With i and j as in the reference program, fill_pattern[a, r, b, c] is 1 exactly when first(i) <= j <= i, for a first column first(i) of tile row i with first(0) = first(1) = 0.
All inputs are finite; a program needn't handle non-finite values.
Results may differ from the reference program's by a relative error of at most 0.0062.
Values may be sent and summed in bfloat16 or wider, within the bound.
No kernel may reach another device: no remote copies, remote signals or barrier semaphores. Data moves between devices by JAX's collectives and lax.ppermute only.
A program may use at most 64 MiB of HBM per device.

```python
import jax
import jax.numpy as jnp

B = 256
S = 512
TR = 4
TC = 2
NT = 128
NCOL = 16
N_ROW = 32
N_COL = 8


def draw_fill_pattern(key, part):
    rows_per = NT // TR
    cols_per = NCOL // TC
    tile_rows = jnp.arange(TR)[:, None] * rows_per + jnp.arange(rows_per)[None, :]
    tile_cols = jnp.arange(TC)[:, None] * cols_per + jnp.arange(cols_per)[None, :]
    key_coin, key_first = jax.random.split(jax.random.fold_in(key, 7))
    coin_flip = jax.random.randint(key_coin, (TR, rows_per), 0, 2)
    start_col = jax.random.randint(key_first, (TR, rows_per), 0, tile_rows + 1)
    first_col = jnp.where((coin_flip == 0) | (tile_rows < 2), 0, start_col)
    row_grid = tile_rows[:, :, None, None]
    col_grid = tile_cols[None, None, :, :]
    inside = (col_grid >= first_col[:, :, None, None]) & (col_grid <= row_grid)
    return inside.astype(jnp.int32)


def draw_w_inverse(key, part):
    key_rows, key_cols = jax.random.split(jax.random.fold_in(key, 11))
    index_line = jnp.arange(B)
    parity = jnp.zeros((B, B), jnp.int32)
    bit_count = B.bit_length() - 1
    for bit_pos in range(bit_count):
        stride = 2 ** bit_pos
        parity = parity + index_line[:, None] // stride % 2 * (index_line[None, :] // stride % 2)
    signed_table = (1 - 2 * (parity % 2)).astype(jnp.float32)
    row_signs = (2 * jax.random.randint(key_rows, (2, B, 1), 0, 2) - 1).astype(jnp.float32)
    col_signs = (2 * jax.random.randint(key_cols, (2, 1, B), 0, 2) - 1).astype(jnp.float32)
    magnitude = 0.25 / jnp.sqrt(jnp.float32(B))
    return (signed_table[None, :, :] * row_signs * col_signs * magnitude).astype(jnp.bfloat16)


def shard_levels(own_key, dims, cuts, least, high):
    def one(axis_at, parts):
        steps = jax.random.uniform(jax.random.fold_in(jax.random.fold_in(own_key, 6), axis_at), (parts,), jnp.float32, least / len(cuts), high / len(cuts))
        return jnp.repeat(jnp.exp(steps), dims[axis_at] // parts).reshape((-1,) + (1,) * (len(dims) - axis_at - 1))

    level = one(*cuts[0])
    for cut in cuts[1:]:
        level = level * one(*cut)
    return level


def centred(own_key, shape, scale, bound, cuts=(), kind=jnp.bfloat16):
    loudness = shard_levels(own_key, shape, cuts, -0.22, 0.18) if cuts else 1.0
    entries = jax.random.normal(own_key, shape, jnp.float32) * scale * loudness
    return jnp.minimum(jnp.maximum(entries, -bound), bound).astype(kind)


def setup_inputs(seed: int = 0) -> dict:
    arg_keys = jax.random.split(jax.random.key(seed), 5)
    return {
        "front_tiles": centred(arg_keys[0], (TR, B * N_ROW, TC, B * N_COL), 1.0, 6.0, ((1, 32), (3, 8))),
        "fill_pattern": draw_fill_pattern(jax.random.fold_in(arg_keys[4], 71), 0),
        "w_inverse": draw_w_inverse(jax.random.fold_in(arg_keys[4], 71), 0),
        "samples": centred(arg_keys[3], (TR, B * N_ROW, S), 1.0, 6.0, ((1, 32),)),
    }


def reference(front_tiles, fill_pattern, w_inverse, samples):
    tiled_view = front_tiles.reshape(TR, N_ROW, B, TC, N_COL, B)
    pattern = fill_pattern.reshape(TR, N_ROW, 1, TC, N_COL, 1).astype(front_tiles.dtype)
    masked = tiled_view * pattern
    tile_row = (jnp.arange(TR)[:, None] * N_ROW + jnp.arange(N_ROW)[None, :]).reshape(NT)
    first_col = masked[:, :, :, 0, 0, :].reshape(NT, B, B)
    second_col = masked[:, :, :, 0, 1, :].reshape(NT, B, B)
    inverse_first = w_inverse[0].astype(jnp.float32)
    inverse_second = w_inverse[1].astype(jnp.float32)
    first_panel = jnp.einsum("ikm,mn->ikn", first_col.astype(jnp.float32), inverse_first)
    first_panel = jnp.where(tile_row[:, None, None] >= 1, first_panel, 0.0).astype(jnp.bfloat16)
    updated_second = second_col.astype(jnp.float32) - jnp.einsum(
        "ikm,nm->ikn", first_panel.astype(jnp.float32), first_panel[1].astype(jnp.float32))
    updated_second = updated_second.astype(jnp.bfloat16)
    second_panel = jnp.einsum("ikm,mn->ikn", updated_second.astype(jnp.float32), inverse_second)
    second_panel = jnp.where(tile_row[:, None, None] >= 2, second_panel, 0.0).astype(jnp.bfloat16)
    both_rows = jnp.concatenate([first_panel, second_panel], axis=2)
    both_cols = both_rows[:NCOL].reshape(TC, N_COL, B, 2 * B).astype(jnp.float32)
    rows_view = both_rows.reshape(TR, N_ROW, B, 2 * B)
    blocks = []
    for group_idx in range(TR):
        rows_here = rows_view[group_idx].astype(jnp.float32)
        product = jnp.einsum("rkm,bcnm->rkbcn", rows_here, both_cols)
        block_out = (masked[group_idx].astype(jnp.float32) - product) * pattern[group_idx].astype(jnp.float32)
        blocks.append(block_out.astype(jnp.bfloat16))
    trailing = jnp.stack(blocks)
    lead_first = jnp.where(tile_row[:, None, None] >= 1, first_panel, first_col)
    lead_second = jnp.where(tile_row[:, None, None] >= 2, second_panel, updated_second)
    trailing = trailing.at[:, :, :, 0, 0, :].set(lead_first.reshape(TR, N_ROW, B, B))
    trailing = trailing.at[:, :, :, 0, 1, :].set(lead_second.reshape(TR, N_ROW, B, B))
    factor_slab = trailing.reshape(TR, N_ROW * B, TC, N_COL * B)

    rhs_tiles = samples.reshape(NT, B, S)
    first_solve = jnp.dot(w_inverse[0].T, rhs_tiles[0], preferred_element_type=jnp.float32).astype(jnp.bfloat16)
    reduced = (rhs_tiles[1].astype(jnp.float32)
               - jnp.dot(first_panel[1], first_solve, preferred_element_type=jnp.float32)).astype(jnp.bfloat16)
    second_solve = jnp.dot(w_inverse[1].T, reduced, preferred_element_type=jnp.float32).astype(jnp.bfloat16)
    stacked = jnp.concatenate([first_solve, second_solve], axis=0).astype(jnp.float32)
    remaining = rhs_tiles.astype(jnp.float32) - jnp.einsum("ikm,ms->iks", both_rows.astype(jnp.float32), stacked)
    remaining = remaining.astype(jnp.bfloat16)
    remaining = remaining.at[0].set(first_solve)
    remaining = remaining.at[1].set(second_solve)
    solved_rows = remaining.reshape(TR, N_ROW * B, S)
    return (factor_slab, solved_rows)
```

```python
import jax
import jax.numpy as jnp
from jax import lax
from jax.sharding import Mesh, PartitionSpec as P

X, Z, Y, K = 4, 8, 4, 2
T = 256
Q = X * Y
RB = T // Q


def halves(tile):
    return tile.reshape(T, 2, T).transpose(1, 0, 2)


def swap(v):
    return lax.ppermute(v, "core", [(0, 1), (1, 0)])


def dotf(eq, a, b):
    return jnp.einsum(eq, a, b, preferred_element_type=jnp.float32)


def body(front, fill, w, samples):
    x = lax.axis_index("x")
    z = lax.axis_index("z")
    y = lax.axis_index("y")
    k = lax.axis_index("core")
    row_pos = x * Z + z
    col_pos = y * K + k
    tile_row = jnp.arange(4) * (X * Z) + row_pos
    pattern = fill.astype(jnp.bfloat16)
    masked = front * pattern
    panel = masked[:, :, 0, :]

    sample_rows = lax.dynamic_index_in_dim(
        halves(samples[0]).reshape(2, Q, K, RB // K, T), k, 2, keepdims=False
    )
    sample_rows = sample_rows.transpose(1, 0, 2, 3).reshape(Q, RB, T)
    send = jnp.concatenate([panel[0].reshape(Q, RB, T), sample_rows], axis=1)
    got = lax.all_to_all(send, ("x", "y"), 0, 0)

    moved = [lax.ppermute(panel, "y", [(0, to)]) for to in (1, 2, 3)]

    send = jnp.concatenate([got[0, :RB], got[Y, :RB], got[0, RB:]], axis=0)
    got = lax.all_to_all(jnp.broadcast_to(send[None], (Z,) + send.shape), "z", 0, 0)

    pairs = got.reshape(Y, 2, 3 * RB, T)[:, :, : 2 * RB, :].reshape(Y, 4 * RB, T)
    common = jnp.concatenate([got[1, :RB], got[0, 2 * RB :], got[1, 2 * RB :]], axis=0)
    send = jnp.concatenate([pairs, jnp.broadcast_to(common[None], (Y,) + common.shape)], axis=1)
    send = jnp.broadcast_to(send[None], (X,) + send.shape).reshape(Q, 7 * RB, T)
    got = lax.all_to_all(send, ("x", "y"), 0, 0)
    cols = got[:, : 4 * RB].reshape(Q, 2, 2, RB, T).transpose(1, 2, 0, 3, 4).reshape(2, 2, T, T)
    tile_one = got[:, 4 * RB : 5 * RB].reshape(T, T)
    samp = got[:, 5 * RB :].reshape(Q, 2, 2, RB // K, T).transpose(1, 0, 3, 2, 4).reshape(2, T // 2, 2 * T)

    own_rows = jnp.where(y == 0, panel, moved[0] + moved[1] + moved[2])
    mine = lax.dynamic_index_in_dim(cols, k, 0, keepdims=False)
    theirs = lax.dynamic_index_in_dim(cols, 1 - k, 0, keepdims=False)
    rows_o, cols_o, one_o, samp_o = swap(own_rows), swap(theirs), swap(tile_one), swap(samp)
    first = k == 0
    rows0 = jnp.where(first, own_rows, rows_o)
    rows1 = jnp.where(first, rows_o, own_rows)
    cols0 = jnp.where(first, mine, cols_o)
    cols1 = jnp.where(first, cols_o, mine)
    one = jnp.where(first, tile_one, one_o)
    samp_lo = jnp.where(first, samp, samp_o).reshape(2, Q, RB // K, 2 * T)
    samp_hi = jnp.where(first, samp_o, samp).reshape(2, Q, RB // K, 2 * T)
    samp = jnp.stack([samp_lo, samp_hi], axis=2).reshape(2, T, 2 * T)

    def panels(f0, f1, index):
        at = index[:, None, None]
        l0 = jnp.where(at >= 1, dotf("akm,mn->akn", f0, w[0]), 0.0).astype(jnp.bfloat16)
        u1 = (f1.astype(jnp.float32) - dotf("akm,nm->akn", l0, l0_one)).astype(jnp.bfloat16)
        l1 = jnp.where(at >= 2, dotf("akm,mn->akn", u1, w[1]), 0.0).astype(jnp.bfloat16)
        return l0, u1, l1

    l0_one = dotf("km,mn->kn", one, w[0]).astype(jnp.bfloat16)
    l0, u1, l1 = panels(rows0, rows1, tile_row)
    c0, _, c1 = panels(cols0, cols1, jnp.arange(2) * (Y * K) + col_pos)
    both_rows = jnp.concatenate([l0, l1], axis=2)
    both_cols = jnp.concatenate([c0, c1], axis=2)
    product = dotf("akm,bnm->akbn", both_rows, both_cols)
    trailing = ((masked.astype(jnp.float32) - product) * pattern.astype(jnp.float32)).astype(jnp.bfloat16)
    first_lead = jnp.where(tile_row[:, None, None] >= 1, l0, rows0)
    second_lead = jnp.where(tile_row[:, None, None] >= 2, l1, u1)
    lead = jnp.where(
        col_pos == 0, first_lead, jnp.where(col_pos == 1, second_lead, trailing[:, :, 0, :])
    )
    slab = jnp.stack([lead, trailing[:, :, 1, :]], axis=2)

    y0 = dotf("mn,ms->ns", w[0], samp[0]).astype(jnp.bfloat16)
    r1 = (samp[1].astype(jnp.float32) - dotf("km,ms->ks", l0_one, y0)).astype(jnp.bfloat16)
    y1 = dotf("mn,ms->ns", w[1], r1).astype(jnp.bfloat16)
    stacked = jnp.concatenate([y0, y1], axis=0)
    remaining = (samples.astype(jnp.float32) - dotf("akm,ms->aks", both_rows, stacked)).astype(jnp.bfloat16)
    top = jnp.where(row_pos == 0, y0, jnp.where(row_pos == 1, y1, remaining[0]))
    solved = jnp.concatenate([top[None], remaining[1:]], axis=0)
    return slab, solved


def solution(mesh):
    fine = Mesh(mesh.devices.reshape(X, Z, Y, K), ("x", "z", "y", "core"))
    row, col = ("x", "z"), ("y", "core")
    in_specs = (P(None, row, None, col), P(None, row, None, col), P(), P(None, row))
    out_specs = (P(None, row, None, col), P(None, row))
    return jax.shard_map(body, mesh=fine, in_specs=in_specs, out_specs=out_specs, check_vma=False)
```

```python
import jax
import jax.numpy as jnp
from jax import lax
from jax.experimental import pallas as pl
from jax.experimental.pallas import tpu as pltpu
from jax.sharding import Mesh, PartitionSpec as P


X, Z, Y, K = 4, 8, 4, 2
T = 256
TR = 4
TC = 2
Q = X * Y
RB = T // Q
F32, BF16 = jnp.float32, jnp.bfloat16


def swap(v):
    return lax.ppermute(v, "core", [(0, 1), (1, 0)])


def mm(a, b):
    return lax.dot_general(a, b, (((1,), (0,)), ((), ())), preferred_element_type=F32)


def mmt(a, b):
    return lax.dot_general(a, b, (((1,), (1,)), ((), ())), preferred_element_type=F32)


def keep(cond, value):
    return jnp.where(cond, value, jnp.zeros_like(value))


def finish(k, place, fill, f0, f1, g0, g1, w, wt, m, samples, slab, solved, lrow, lcol, ys, obuf, sem):
    row_pos = place[0]
    col_pos = place[1]

    def tile(ref, at):
        return ref[:, at * RB : (at + 1) * RB, :].reshape(T, T)

    l0_one = mm(tile(g0, 4), w[0]).astype(BF16)

    for half, g in enumerate((g0, g1)):
        y0 = mm(wt[0], tile(g, 5)).astype(BF16)
        r1 = (tile(g, 6).astype(F32) - mm(l0_one, y0)).astype(BF16)
        y1 = mm(wt[1], r1).astype(BF16)
        ys[0:T, half * T : (half + 1) * T] = y0
        ys[T : 2 * T, half * T : (half + 1) * T] = y1

    for a in range(TR):
        index = a * X * Z + row_pos
        first = mm(f0[a], w[0]).astype(BF16)
        if a == 0:
            first = keep(index >= 1, first)
        second = (f1[a].astype(F32) - mmt(first, l0_one)).astype(BF16)
        third = mm(second, w[1]).astype(BF16)
        if a == 0:
            third = keep(index >= 2, third)
        lrow[a * T : (a + 1) * T, 0:T] = first
        lrow[a * T : (a + 1) * T, T : 2 * T] = third
        if a == 0:
            slab[0, 0] = second

    for a in range(TR):
        rest = samples[a].astype(F32) - mm(lrow[a * T : (a + 1) * T, :], ys[...])
        obuf[a] = rest.astype(BF16)
        if a == 0:

            @pl.when(row_pos == 0)
            def _():
                obuf[0] = ys[0:T, :]

            @pl.when(row_pos == 1)
            def _():
                obuf[0] = ys[T : 2 * T, :]

        pltpu.make_async_copy(obuf.at[a], solved.at[a], sem.at[a]).start()

    for b in range(TC):
        index = b * Y * K + col_pos
        first = mm(tile(g0, 2 * k + b), w[0]).astype(BF16)
        if b == 0:
            first = keep(index >= 1, first)
        second = (tile(g1, 2 * k + b).astype(F32) - mmt(first, l0_one)).astype(BF16)
        third = mm(second, w[1]).astype(BF16)
        if b == 0:
            third = keep(index >= 2, third)
        lcol[b * T : (b + 1) * T, 0:T] = first
        lcol[b * T : (b + 1) * T, T : 2 * T] = third

    for a in range(TR):
        index = a * X * Z + row_pos
        rows = lrow[a * T : (a + 1) * T, :]
        for b in range(TC):
            if b == 0:

                @pl.when(col_pos == 0)
                def _():
                    slab[0, a] = rows[:, 0:T]

                    if a == 0:

                        @pl.when(index < 1)
                        def _():
                            slab[0, a] = f0[a]

                @pl.when(col_pos == 1)
                def _():
                    if a == 0:

                        @pl.when(index >= 2)
                        def _():
                            slab[0, a] = rows[:, T : 2 * T]

                    else:
                        slab[0, a] = rows[:, T : 2 * T]

                @pl.when(col_pos >= 2)
                def _():
                    rest = m[0, a].astype(F32) - mmt(rows, lcol[0:T, :])
                    slab[0, a] = keep(fill[2 * a] != 0, rest.astype(BF16))

            else:
                rest = m[b, a].astype(F32) - mmt(rows, lcol[b * T : (b + 1) * T, :])
                slab[b, a] = keep(fill[2 * a + b] != 0, rest.astype(BF16))

    for a in range(TR):
        pltpu.make_async_copy(obuf.at[a], solved.at[a], sem.at[a]).wait()


def finish_kernel(place, fill, own, other, got, got_o, w, wt, m, samples, *rest):
    @pl.when(place[2] == 0)
    def _():
        finish(0, place, fill, own, other, got, got_o, w, wt, m, samples, *rest)

    @pl.when(place[2] == 1)
    def _():
        finish(1, place, fill, other, own, got_o, got, w, wt, m, samples, *rest)


def body(front, fill, w, samples):
    x = lax.axis_index("x")
    z = lax.axis_index("z")
    y = lax.axis_index("y")
    k = lax.axis_index("core")
    masked = front * fill.astype(BF16)
    panel = masked[:, :, 0, :]

    piece = lax.dynamic_slice_in_dim(samples[0], k * T, T, 1)
    send = jnp.concatenate([panel[0].reshape(Q, RB, T), piece.reshape(Q, RB, T)], axis=1)
    got = lax.all_to_all(send, ("x", "y"), 0, 0)

    moved = []
    for to in (1, 2, 3):
        moved.append(lax.ppermute(panel, "y", [(0, to)]))

    send = jnp.concatenate([got[0, :RB], got[Y, :RB], got[0, RB:]], axis=0)
    got = lax.all_to_all(jnp.broadcast_to(send[None], (Z,) + send.shape), "z", 0, 0)

    pairs = got.reshape(Y, 2, 3 * RB, T)[:, :, : 2 * RB, :].reshape(Y, 4 * RB, T)
    common = jnp.concatenate([got[1, :RB], got[0, 2 * RB :], got[1, 2 * RB :]], axis=0)
    send = jnp.concatenate([pairs, jnp.broadcast_to(common[None], (Y,) + common.shape)], axis=1)
    send = jnp.broadcast_to(send[None], (X,) + send.shape).reshape(Q, 7 * RB, T)
    got = lax.all_to_all(send, ("x", "y"), 0, 0)

    own = lax.select(y == 0, panel, moved[0] + moved[1] + moved[2])
    other = swap(own)
    got_o = swap(got)

    place = jnp.stack([x * Z + z, y * K + k, k]).astype(jnp.int32)
    vmem = pl.BlockSpec(memory_space=pltpu.VMEM)
    smem = pl.BlockSpec(memory_space=pltpu.SMEM)
    slab, solved = pl.pallas_call(
        finish_kernel,
        in_specs=[smem, smem] + [vmem] * 8,
        out_specs=[vmem, pl.BlockSpec(memory_space=pl.ANY)],
        out_shape=[
            jax.ShapeDtypeStruct((TC, TR, T, T), BF16),
            jax.ShapeDtypeStruct((TR, T, 2 * T), BF16),
        ],
        scratch_shapes=[
            pltpu.VMEM((TR * T, 2 * T), BF16),
            pltpu.VMEM((TC * T, 2 * T), BF16),
            pltpu.VMEM((2 * T, 2 * T), BF16),
            pltpu.VMEM((TR, T, 2 * T), BF16),
            pltpu.SemaphoreType.DMA((TR,)),
        ],
        compiler_params=pltpu.CompilerParams(vmem_limit_bytes=20 * 1024 * 1024),
        name="finish",
    )(
        place,
        fill.reshape(TR * TC),
        own,
        other,
        got,
        got_o,
        w,
        w.transpose(0, 2, 1),
        masked.transpose(2, 0, 1, 3),
        samples,
    )
    return slab.transpose(1, 2, 0, 3), solved


def solution(mesh):
    fine = Mesh(mesh.devices.reshape(X, Z, Y, K), ("x", "z", "y", "core"))
    row, col = ("x", "z"), ("y", "core")
    in_specs = (P(None, row, None, col), P(None, row, None, col), P(), P(None, row))
    out_specs = (P(None, row, None, col), P(None, row))
    return jax.shard_map(body, mesh=fine, in_specs=in_specs, out_specs=out_specs, check_vma=False)
```

```python
import jax
import jax.numpy as jnp
from jax import lax
from jax.experimental import pallas as pl
from jax.experimental.pallas import tpu as pltpu
from jax.sharding import Mesh, PartitionSpec as P


X, Z, Y, K = 4, 8, 4, 2
T = 256
TR = 4
TC = 2
Q = X * Y
RB = T // Q
F32, BF16 = jnp.float32, jnp.bfloat16


def swap(v):
    return lax.ppermute(v, "core", [(0, 1), (1, 0)])


def mm(a, b):
    return lax.dot_general(a, b, (((1,), (0,)), ((), ())), preferred_element_type=F32)


def mmt(a, b):
    return lax.dot_general(a, b, (((1,), (1,)), ((), ())), preferred_element_type=F32)


def tmm(a, b):
    return lax.dot_general(a, b, (((0,), (0,)), ((), ())), preferred_element_type=F32)


def keep(cond, value):
    return jnp.where(cond, value, jnp.zeros_like(value))


def finish(k, place, f0, f1, g0, g1, wt, m, samples, slab, solved, lrow, lcol, ys, obuf, sem, arrival):
    row_pos = place[0]
    col_pos = place[1]

    def tile(ref, at):
        return ref[:, at * RB : (at + 1) * RB, :].reshape(T, T)

    def pair(ref, at):
        return jnp.concatenate([tile(ref, at), tile(ref, at + 1)], axis=0)

    l0_one = mm(tile(g0, 4), wt[0]).astype(BF16)

    lcol[:, 0:T] = mm(pair(g0, 2 * k), wt[0]).astype(BF16)

    @pl.when(col_pos == 0)
    def _():
        lcol[0:T, 0:T] = jnp.zeros((T, T), BF16)

    second = (pair(g1, 2 * k).astype(F32) - mmt(lcol[:, 0:T], l0_one)).astype(BF16)
    lcol[:, T : 2 * T] = mm(second, wt[1]).astype(BF16)

    y0 = tmm(wt[0], jnp.concatenate([tile(g0, 5), tile(g1, 5)], axis=1)).astype(BF16)
    r1 = jnp.concatenate([tile(g0, 6), tile(g1, 6)], axis=1).astype(F32) - mm(l0_one, y0)
    ys[0:T, :] = y0
    ys[T : 2 * T, :] = tmm(wt[1], r1.astype(BF16)).astype(BF16)

    arrival.wait()
    lrow[:, 0:T] = mm(f0[...].reshape(TR * T, T), wt[0]).astype(BF16)

    @pl.when(row_pos == 0)
    def _():
        lrow[0:T, 0:T] = jnp.zeros((T, T), BF16)

    second = (f1[...].reshape(TR * T, T).astype(F32) - mmt(lrow[:, 0:T], l0_one)).astype(BF16)
    lrow[:, T : 2 * T] = mm(second, wt[1]).astype(BF16)
    slab[0, 0] = second[0:T]

    @pl.when(row_pos <= 1)
    def _():
        lrow[0:T, T : 2 * T] = jnp.zeros((T, T), BF16)

    @pl.when(col_pos <= 1)
    def _():
        lcol[0:T, T : 2 * T] = jnp.zeros((T, T), BF16)

    for a in range(TR):
        rest = samples[a].astype(F32) - mm(lrow[a * T : (a + 1) * T, :], ys[...])
        obuf[a] = rest.astype(BF16)

    @pl.when(row_pos == 0)
    def _():
        obuf[0] = ys[0:T, :]

    @pl.when(row_pos == 1)
    def _():
        obuf[0] = ys[T : 2 * T, :]

    out = pltpu.make_async_copy(obuf, solved, sem)
    out.start()

    for a in range(TR):
        product = mmt(lrow[a * T : (a + 1) * T, :], lcol[...])
        for b in range(TC):
            rest = (m[b, a].astype(F32) - product[:, b * T : (b + 1) * T]).astype(BF16)
            rest = keep(place[3 + 2 * a + b] != 0, rest)
            if (a, b) == (0, 0):
                @pl.when(col_pos >= 2)
                def _():
                    slab[0, 0] = rest

            else:
                slab[b, a] = rest

    @pl.when(col_pos == 0)
    def _():
        for a in range(1, TR):
            slab[0, a] = lrow[a * T : (a + 1) * T, 0:T]

        @pl.when(row_pos == 0)
        def _():
            slab[0, 0] = f0[0]

        @pl.when(row_pos >= 1)
        def _():
            slab[0, 0] = lrow[0:T, 0:T]

    @pl.when(col_pos == 1)
    def _():
        for a in range(1, TR):
            slab[0, a] = lrow[a * T : (a + 1) * T, T : 2 * T]

        @pl.when(row_pos >= 2)
        def _():
            slab[0, 0] = lrow[0:T, T : 2 * T]

    out.wait()


def finish_kernel(place, own, other_hbm, got, got_o, wt, m, samples, *rest):
    *rest, other, other_sem = rest
    arrival = pltpu.make_async_copy(other_hbm, other, other_sem)
    arrival.start()
    rest = (*rest, arrival)

    @pl.when(place[2] == 0)
    def _():
        finish(0, place, own, other, got, got_o, wt, m, samples, *rest)

    @pl.when(place[2] == 1)
    def _():
        finish(1, place, other, own, got_o, got, wt, m, samples, *rest)


def body(front, fill, w, samples):
    x = lax.axis_index("x")
    z = lax.axis_index("z")
    y = lax.axis_index("y")
    k = lax.axis_index("core")
    tiles = front.transpose(2, 0, 1, 3)
    pattern = fill.astype(BF16)[:, :, 0, :]
    panel = tiles[0] * pattern

    piece = lax.dynamic_slice(samples, (0, 0, k * T), (1, T, T))
    send = jnp.concatenate([(tiles[0, 0] * pattern[0]).reshape(Q, RB, T), piece.reshape(Q, RB, T)], axis=1)
    got = lax.all_to_all(send, ("x", "y"), 0, 0)

    moved = []
    for to in (1, 2, 3):
        moved.append(lax.ppermute(panel, "y", [(0, to)]))

    send = jnp.concatenate([got[0, :RB], got[Y, :RB], got[0, RB:]], axis=0)
    got = lax.all_to_all(jnp.broadcast_to(send[None], (Z,) + send.shape), "z", 0, 0)

    pairs = got.reshape(Y, 2, 3 * RB, T)[:, :, : 2 * RB, :].reshape(Y, 4 * RB, T)
    common = jnp.concatenate([got[1, :RB], got[0, 2 * RB :], got[1, 2 * RB :]], axis=0)
    send = jnp.concatenate([pairs, jnp.broadcast_to(common[None], (Y,) + common.shape)], axis=1)
    send = jnp.broadcast_to(send[None], (X,) + send.shape).reshape(Q, 7 * RB, T)
    got = lax.all_to_all(send, ("x", "y"), 0, 0)

    wt = w * jnp.where(z >= 0, 1.0, 0.0).astype(BF16)
    place = jnp.stack([x * Z + z, y * K + k, k]).astype(jnp.int32)
    place = jnp.concatenate([place, fill.reshape(TR * TC)])

    own = lax.select(y == 0, panel, moved[0] + moved[1] + moved[2])
    other = swap(own)
    got_o = swap(got)

    vmem = pl.BlockSpec(memory_space=pltpu.VMEM)
    smem = pl.BlockSpec(memory_space=pltpu.SMEM)
    slab, solved = pl.pallas_call(
        finish_kernel,
        in_specs=[smem, vmem, pl.BlockSpec(memory_space=pl.ANY)] + [vmem] * 5,
        out_specs=[vmem, pl.BlockSpec(memory_space=pl.ANY)],
        out_shape=[
            jax.ShapeDtypeStruct((TC, TR, T, T), BF16),
            jax.ShapeDtypeStruct((TR, T, 2 * T), BF16),
        ],
        scratch_shapes=[
            pltpu.VMEM((TR * T, 2 * T), BF16),
            pltpu.VMEM((TC * T, 2 * T), BF16),
            pltpu.VMEM((2 * T, 2 * T), BF16),
            pltpu.VMEM((TR, T, 2 * T), BF16),
            pltpu.SemaphoreType.DMA,
            pltpu.VMEM((TR, T, T), BF16),
            pltpu.SemaphoreType.DMA,
        ],
        compiler_params=pltpu.CompilerParams(vmem_limit_bytes=20 * 1024 * 1024),
        name="finish",
    )(
        place,
        own,
        other,
        got,
        got_o,
        wt,
        tiles,
        samples,
    )
    return slab.transpose(1, 2, 0, 3), solved


def solution(mesh):
    fine = Mesh(mesh.devices.reshape(X, Z, Y, K), ("x", "z", "y", "core"))
    row, col = ("x", "z"), ("y", "core")
    in_specs = (P(None, row, None, col), P(None, row, None, col), P(), P(None, row))
    out_specs = (P(None, row, None, col), P(None, row))
    return jax.shard_map(body, mesh=fine, in_specs=in_specs, out_specs=out_specs, check_vma=False)
```

```python
import jax
import jax.numpy as jnp
from jax import lax
from jax.experimental import pallas as pl
from jax.experimental.pallas import tpu as pltpu
from jax.sharding import Mesh, PartitionSpec as P


X, Z, Y, K = 4, 8, 4, 2
T = 256
TR = 4
TC = 2
Q = X * Y
RB = T // Q
F32, BF16 = jnp.float32, jnp.bfloat16


def swap(v):
    return lax.ppermute(v, "core", [(0, 1), (1, 0)])


def mm(a, b):
    return lax.dot_general(a, b, (((1,), (0,)), ((), ())), preferred_element_type=F32)


def mmt(a, b):
    return lax.dot_general(a, b, (((1,), (1,)), ((), ())), preferred_element_type=F32)


def tmm(a, b):
    return lax.dot_general(a, b, (((0,), (0,)), ((), ())), preferred_element_type=F32)


def keep(cond, value):
    return jnp.where(cond, value, jnp.zeros_like(value))


def finish(k, place, f0, f1, g0, g1, w, m, samples, slab, solved, lrow, lcol, ys, obuf, sem, arrival):
    row_pos = place[0]
    col_pos = place[1]

    def tile(ref, at):
        return ref[:, at * RB : (at + 1) * RB, :].reshape(T, T)

    def from_second(tile_second, first):
        return (tile_second.astype(F32) - mmt(first, l0_one)).astype(BF16)

    l0_one = mm(tile(g0, 4), w[0]).astype(BF16)
    first_col = [mm(tile(g0, 2 * k + b), w[0]).astype(BF16) for b in range(TC)]
    first_col[0] = keep(col_pos >= 1, first_col[0])
    y0 = tmm(w[0], jnp.concatenate([tile(g0, 5), tile(g1, 5)], axis=1)).astype(BF16)
    arrival.wait()
    first_row = mm(f0[...].reshape(TR * T, T), w[0]).astype(BF16)
    first_row = [first_row[a * T : (a + 1) * T] for a in range(TR)]
    first_row[0] = keep(row_pos >= 1, first_row[0])
    ys[0:T, :] = y0
    for b in range(TC):
        lcol[b * T : (b + 1) * T, 0:T] = first_col[b]
    for a in range(TR):
        lrow[a * T : (a + 1) * T, 0:T] = first_row[a]

    second_col = [from_second(tile(g1, 2 * k + b), first_col[b]) for b in range(TC)]
    second_row = [from_second(f1[a], first_row[a]) for a in range(TR)]
    r1 = jnp.concatenate([tile(g0, 6), tile(g1, 6)], axis=1).astype(F32) - mm(l0_one, y0)
    slab[0, 0] = second_row[0]
    for b in range(TC):
        third = mm(second_col[b], w[1]).astype(BF16)
        lcol[b * T : (b + 1) * T, T : 2 * T] = keep(col_pos >= 2, third) if b == 0 else third
    for a in range(TR):
        third = mm(second_row[a], w[1]).astype(BF16)
        lrow[a * T : (a + 1) * T, T : 2 * T] = keep(row_pos >= 2, third) if a == 0 else third
    ys[T : 2 * T, :] = tmm(w[1], r1.astype(BF16)).astype(BF16)

    for a in range(TR):
        rows = lrow[a * T : (a + 1) * T, :]
        obuf[a] = (samples[a].astype(F32) - mm(rows, ys[...])).astype(BF16)

    @pl.when(row_pos == 0)
    def _():
        obuf[0] = ys[0:T, :]

    @pl.when(row_pos == 1)
    def _():
        obuf[0] = ys[T : 2 * T, :]

    out = pltpu.make_async_copy(obuf, solved, sem)
    out.start()

    for a in range(TR):
        product = mmt(lrow[a * T : (a + 1) * T, :], lcol[...])
        for b in range(TC):
            rest = (m[b, a].astype(F32) - product[:, b * T : (b + 1) * T]).astype(BF16)
            rest = keep(place[3 + 2 * a + b] != 0, rest)
            slab[b, a] = lax.select(col_pos >= 2, rest, slab[0, 0]) if (a, b) == (0, 0) else rest

    @pl.when(col_pos == 0)
    def _():
        for a in range(1, TR):
            slab[0, a] = lrow[a * T : (a + 1) * T, 0:T]

        @pl.when(row_pos == 0)
        def _():
            slab[0, 0] = f0[0]

        @pl.when(row_pos >= 1)
        def _():
            slab[0, 0] = lrow[0:T, 0:T]

    @pl.when(col_pos == 1)
    def _():
        for a in range(1, TR):
            slab[0, a] = lrow[a * T : (a + 1) * T, T : 2 * T]

        @pl.when(row_pos >= 2)
        def _():
            slab[0, 0] = lrow[0:T, T : 2 * T]

    out.wait()


def finish_kernel(place, own, other_hbm, got, got_o, wt, m, samples, *rest):
    *rest, other, other_sem = rest
    arrival = pltpu.make_async_copy(other_hbm, other, other_sem)
    arrival.start()
    rest = (*rest, arrival)

    @pl.when(place[2] == 0)
    def _():
        finish(0, place, own, other, got, got_o, wt, m, samples, *rest)

    @pl.when(place[2] == 1)
    def _():
        finish(1, place, other, own, got_o, got, wt, m, samples, *rest)


def body(front, fill, w, samples):
    x = lax.axis_index("x")
    z = lax.axis_index("z")
    y = lax.axis_index("y")
    k = lax.axis_index("core")
    tiles = front.transpose(2, 0, 1, 3) * fill.astype(BF16).transpose(2, 0, 1, 3)
    tiles = lax.optimization_barrier(tiles)
    panel = tiles[0]

    piece = lax.dynamic_slice(samples, (0, 0, k * T), (1, T, T))
    send = jnp.concatenate([panel[0].reshape(Q, RB, T), piece.reshape(Q, RB, T)], axis=1)
    got = lax.all_to_all(send, ("x", "y"), 0, 0)

    right = lax.ppermute(panel, "y", [(0, 1)])
    left = lax.ppermute(panel, "y", [(0, 3)])
    lower = lax.ppermute(right[: TR // 2], "y", [(1, 2)])
    upper = lax.ppermute(left[TR // 2 :], "y", [(3, 2)])

    send = jnp.concatenate([got[0, :RB], got[Y, :RB], got[0, RB:]], axis=0)
    got = lax.all_to_all(jnp.broadcast_to(send[None], (Z,) + send.shape), "z", 0, 0)

    pairs = got.reshape(Y, 2, 3 * RB, T)[:, :, : 2 * RB, :].reshape(Y, 4 * RB, T)
    common = jnp.concatenate([got[1, :RB], got[0, 2 * RB :], got[1, 2 * RB :]], axis=0)
    send = jnp.concatenate([pairs, jnp.broadcast_to(common[None], (Y,) + common.shape)], axis=1)
    send = jnp.broadcast_to(send[None], (X,) + send.shape).reshape(Q, 7 * RB, T)
    got = lax.all_to_all(send, ("x", "y"), 0, 0)

    wt = w * jnp.where(z >= 0, 1.0, 0.0).astype(BF16)
    place = jnp.stack([x * Z + z, y * K + k, k]).astype(jnp.int32)
    place = jnp.concatenate([place, fill.reshape(TR * TC)])

    own = lax.select(y == 0, panel, right + left + jnp.concatenate([lower, upper]))
    other = swap(own)
    got_o = swap(got)

    vmem = pl.BlockSpec(memory_space=pltpu.VMEM)
    smem = pl.BlockSpec(memory_space=pltpu.SMEM)
    slab, solved = pl.pallas_call(
        finish_kernel,
        in_specs=[smem, vmem, pl.BlockSpec(memory_space=pl.ANY)] + [vmem] * 5,
        out_specs=[vmem, pl.BlockSpec(memory_space=pl.ANY)],
        out_shape=[
            jax.ShapeDtypeStruct((TC, TR, T, T), BF16),
            jax.ShapeDtypeStruct((TR, T, 2 * T), BF16),
        ],
        scratch_shapes=[
            pltpu.VMEM((TR * T, 2 * T), BF16),
            pltpu.VMEM((TC * T, 2 * T), BF16),
            pltpu.VMEM((2 * T, 2 * T), BF16),
            pltpu.VMEM((TR, T, 2 * T), BF16),
            pltpu.SemaphoreType.DMA,
            pltpu.VMEM((TR, T, T), BF16),
            pltpu.SemaphoreType.DMA,
        ],
        compiler_params=pltpu.CompilerParams(vmem_limit_bytes=20 * 1024 * 1024),
        name="finish",
    )(
        place,
        own,
        other,
        got,
        got_o,
        wt,
        tiles,
        samples,
    )
    return slab.transpose(1, 2, 0, 3), solved


def solution(mesh):
    fine = Mesh(mesh.devices.reshape(X, Z, Y, K), ("x", "z", "y", "core"))
    row, col = ("x", "z"), ("y", "core")
    in_specs = (P(None, row, None, col), P(None, row, None, col), P(), P(None, row))
    out_specs = (P(None, row, None, col), P(None, row))
    return jax.shard_map(body, mesh=fine, in_specs=in_specs, out_specs=out_specs, check_vma=False)
```

```python
import jax
import jax.numpy as jnp
from jax import lax
from jax.experimental import pallas as pl
from jax.experimental.pallas import tpu as pltpu
from jax.sharding import Mesh, PartitionSpec as P


X, Z, Y, K = 4, 8, 4, 2
T = 256
TR = 4
TC = 2
Q = X * Y
RB = T // Q
F32, BF16 = jnp.float32, jnp.bfloat16


def swap(v):
    return lax.ppermute(v, "core", [(0, 1), (1, 0)])


def mm(a, b):
    return lax.dot_general(a, b, (((1,), (0,)), ((), ())), preferred_element_type=F32)


def mmt(a, b):
    return lax.dot_general(a, b, (((1,), (1,)), ((), ())), preferred_element_type=F32)


def tmm(a, b):
    return lax.dot_general(a, b, (((0,), (0,)), ((), ())), preferred_element_type=F32)


def keep(cond, value):
    return jnp.where(cond, value, jnp.zeros_like(value))


def finish(k, place, f0, f1, g0, g1, m0, m1, samples, slab, solved, lrow, lcol, ys, obuf, sem, arrival):
    row_pos = place[0]
    col_pos = place[1]
    w = (f0[TR], f0[TR + 1])
    m = (m0, m1)

    def tile(ref, at):
        return ref[:, at * RB : (at + 1) * RB, :].reshape(T, T)

    def from_second(tile_second, first):
        return (tile_second.astype(F32) - mmt(first, l0_one)).astype(BF16)

    l0_one = mm(tile(g0, 4), w[0]).astype(BF16)
    first_col = [mm(tile(g0, 2 * k + b), w[0]).astype(BF16) for b in range(TC)]
    first_col[0] = keep(col_pos >= 1, first_col[0])
    y0 = tmm(w[0], jnp.concatenate([tile(g0, 5), tile(g1, 5)], axis=1)).astype(BF16)
    first_row = mm(f0[0:TR].reshape(TR * T, T), w[0]).astype(BF16)
    first_row = [first_row[a * T : (a + 1) * T] for a in range(TR)]
    first_row[0] = keep(row_pos >= 1, first_row[0])
    ys[0:T, :] = y0
    for b in range(TC):
        lcol[b * T : (b + 1) * T, 0:T] = first_col[b]
    for a in range(TR):
        lrow[a * T : (a + 1) * T, 0:T] = first_row[a]

    second_col = [from_second(tile(g1, 2 * k + b), first_col[b]) for b in range(TC)]
    second_row = [from_second(f1[a], first_row[a]) for a in range(TR)]
    r1 = jnp.concatenate([tile(g0, 6), tile(g1, 6)], axis=1).astype(F32) - mm(l0_one, y0)
    slab[0, 0] = second_row[0]
    for b in range(TC):
        third = mm(second_col[b], w[1]).astype(BF16)
        lcol[b * T : (b + 1) * T, T : 2 * T] = keep(col_pos >= 2, third) if b == 0 else third
    for a in range(TR):
        third = mm(second_row[a], w[1]).astype(BF16)
        lrow[a * T : (a + 1) * T, T : 2 * T] = keep(row_pos >= 2, third) if a == 0 else third
    ys[T : 2 * T, :] = tmm(w[1], r1.astype(BF16)).astype(BF16)

    arrival.wait()
    for a in range(TR):
        rows = lrow[a * T : (a + 1) * T, :]
        obuf[a] = (samples[a].astype(F32) - mm(rows, ys[...])).astype(BF16)

    @pl.when(row_pos == 0)
    def _():
        obuf[0] = ys[0:T, :]

    @pl.when(row_pos == 1)
    def _():
        obuf[0] = ys[T : 2 * T, :]

    out = pltpu.make_async_copy(obuf, solved, sem)
    out.start()

    for a in range(TR):
        product = mmt(lrow[a * T : (a + 1) * T, :], lcol[...])
        for b in range(TC):
            rest = (m[b][a].astype(F32) - product[:, b * T : (b + 1) * T]).astype(BF16)
            rest = keep(place[3 + 2 * a + b] != 0, rest)
            slab[b, a] = lax.select(col_pos >= 2, rest, slab[0, 0]) if (a, b) == (0, 0) else rest

    @pl.when(col_pos == 0)
    def _():
        for a in range(1, TR):
            slab[0, a] = lrow[a * T : (a + 1) * T, 0:T]

        @pl.when(row_pos == 0)
        def _():
            slab[0, 0] = f0[0]

        @pl.when(row_pos >= 1)
        def _():
            slab[0, 0] = lrow[0:T, 0:T]

    @pl.when(col_pos == 1)
    def _():
        for a in range(1, TR):
            slab[0, a] = lrow[a * T : (a + 1) * T, T : 2 * T]

        @pl.when(row_pos >= 2)
        def _():
            slab[0, 0] = lrow[0:T, T : 2 * T]

    out.wait()


def finish_kernel(place, rows0, rows1, got, got_o, m0, m1, samples_far, *rest):
    *rest, samples, samples_sem = rest
    arrival = pltpu.make_async_copy(samples_far, samples, samples_sem)
    arrival.start()
    rest = (m0, m1, samples, *rest, arrival)

    @pl.when(place[2] == 0)
    def _():
        finish(0, place, rows0, rows1, got, got_o, *rest)

    @pl.when(place[2] == 1)
    def _():
        finish(1, place, rows0, rows1, got_o, got, *rest)


def body(front, fill, w, samples):
    x = lax.axis_index("x")
    z = lax.axis_index("z")
    y = lax.axis_index("y")
    k = lax.axis_index("core")
    pattern = fill.astype(BF16)
    panel = lax.optimization_barrier(front[:, :, 0, :] * pattern[:, :, 0, :])

    piece = lax.dynamic_slice(samples, (0, 0, k * T), (1, T, T))
    send = jnp.concatenate([panel[0].reshape(Q, RB, T), piece.reshape(Q, RB, T)], axis=1)
    got = lax.all_to_all(send, ("x", "y"), 0, 0)

    right = lax.ppermute(panel, "y", [(0, 1)])
    left = lax.ppermute(panel, "y", [(0, 3)])
    far = lax.ppermute(right, "y", [(1, 2)])

    send = jnp.concatenate([got[0, :RB], got[Y, :RB], got[0, RB:]], axis=0)
    got = lax.all_to_all(jnp.broadcast_to(send[None], (Z,) + send.shape), "z", 0, 0)

    pairs = got.reshape(Y, 2, 3 * RB, T)[:, :, : 2 * RB, :].reshape(Y, 4 * RB, T)
    common = jnp.concatenate([got[1, :RB], got[0, 2 * RB :], got[1, 2 * RB :]], axis=0)
    send = jnp.concatenate([pairs, jnp.broadcast_to(common[None], (Y,) + common.shape)], axis=1)
    send = jnp.broadcast_to(send[None], (X,) + send.shape).reshape(Q, 7 * RB, T)
    got = lax.all_to_all(send, ("x", "y"), 0, 0)

    rest = lax.optimization_barrier(front[:, :, 1, :] * pattern[:, :, 1, :])
    place = jnp.stack([x * Z + z, y * K + k, k]).astype(jnp.int32)
    place = jnp.concatenate([place, fill.reshape(TR * TC)])

    own = lax.select(y == 0, panel, right + left + far)
    other = swap(own)
    rows0 = jnp.concatenate([lax.select(k == 0, own, other), w])
    rows1 = lax.select(k == 0, other, own)
    got_o = swap(got)

    vmem = pl.BlockSpec(memory_space=pltpu.VMEM)
    smem = pl.BlockSpec(memory_space=pltpu.SMEM)
    slab, solved = pl.pallas_call(
        finish_kernel,
        in_specs=[smem] + [vmem] * 6 + [pl.BlockSpec(memory_space=pltpu.HBM)],
        out_specs=[vmem, pl.BlockSpec(memory_space=pl.ANY)],
        out_shape=[
            jax.ShapeDtypeStruct((TC, TR, T, T), BF16),
            jax.ShapeDtypeStruct((TR, T, 2 * T), BF16),
        ],
        scratch_shapes=[
            pltpu.VMEM((TR * T, 2 * T), BF16),
            pltpu.VMEM((TC * T, 2 * T), BF16),
            pltpu.VMEM((2 * T, 2 * T), BF16),
            pltpu.VMEM((TR, T, 2 * T), BF16),
            pltpu.SemaphoreType.DMA,
            pltpu.VMEM((TR, T, 2 * T), BF16),
            pltpu.SemaphoreType.DMA,
        ],
        compiler_params=pltpu.CompilerParams(vmem_limit_bytes=20 * 1024 * 1024),
        name="finish",
    )(
        place,
        rows0,
        rows1,
        got,
        got_o,
        panel,
        rest,
        pltpu.with_memory_space_constraint(samples, pltpu.HBM),
    )
    return slab.transpose(1, 2, 0, 3), solved


def solution(mesh):
    fine = Mesh(mesh.devices.reshape(X, Z, Y, K), ("x", "z", "y", "core"))
    row, col = ("x", "z"), ("y", "core")
    in_specs = (P(None, row, None, col), P(None, row, None, col), P(), P(None, row))
    out_specs = (P(None, row, None, col), P(None, row))
    return jax.shard_map(body, mesh=fine, in_specs=in_specs, out_specs=out_specs, check_vma=False)
```

```python
import jax
import jax.numpy as jnp
from jax import lax
from jax.experimental import pallas as pl
from jax.experimental.pallas import tpu as pltpu
from jax.sharding import Mesh, PartitionSpec as P


X, Z, Y, K = 4, 8, 4, 2
T = 256
TR = 4
TC = 2
Q = X * Y
RB = T // Q
F32, BF16 = jnp.float32, jnp.bfloat16


def swap(v):
    return lax.ppermute(v, "core", [(0, 1), (1, 0)])


def mm(a, b):
    return lax.dot_general(a, b, (((1,), (0,)), ((), ())), preferred_element_type=F32)


def mmt(a, b):
    return lax.dot_general(a, b, (((1,), (1,)), ((), ())), preferred_element_type=F32)


def tmm(a, b):
    return lax.dot_general(a, b, (((0,), (0,)), ((), ())), preferred_element_type=F32)


def keep(cond, value):
    return jnp.where(cond, value, jnp.zeros_like(value))


def finish(k, place, f0, f1, g0, g1, m0, m1, samples, slab, solved, lrow, lcol, ys, obuf, sem, arrival):
    row_pos = place[0]
    col_pos = place[1]
    w = (f0[TR], f0[TR + 1])
    m = (m0, m1)

    def tile(ref, at):
        return ref[:, at * RB : (at + 1) * RB, :].reshape(T, T)

    def from_second(tile_second, first):
        return (tile_second.astype(F32) - mmt(first, l0_one)).astype(BF16)

    l0_one = mm(tile(g0, 4), w[0]).astype(BF16)
    first_col = [mm(tile(g0, 2 * k + b), w[0]).astype(BF16) for b in range(TC)]
    first_col[0] = keep(col_pos >= 1, first_col[0])
    y0 = tmm(w[0], jnp.concatenate([tile(g0, 5), tile(g1, 5)], axis=1)).astype(BF16)
    first_row = mm(f0[0:TR].reshape(TR * T, T), w[0]).astype(BF16)
    first_row = [first_row[a * T : (a + 1) * T] for a in range(TR)]
    first_row[0] = keep(row_pos >= 1, first_row[0])
    ys[0:T, :] = y0
    for b in range(TC):
        lcol[b * T : (b + 1) * T, 0:T] = first_col[b]
    for a in range(TR):
        lrow[a * T : (a + 1) * T, 0:T] = first_row[a]

    second_col = [from_second(tile(g1, 2 * k + b), first_col[b]) for b in range(TC)]
    second_row = [from_second(f1[a], first_row[a]) for a in range(TR)]
    r1 = jnp.concatenate([tile(g0, 6), tile(g1, 6)], axis=1).astype(F32) - mm(l0_one, y0)
    slab[0, 0] = second_row[0]
    for b in range(TC):
        third = mm(second_col[b], w[1]).astype(BF16)
        lcol[b * T : (b + 1) * T, T : 2 * T] = keep(col_pos >= 2, third) if b == 0 else third
    for a in range(TR):
        third = mm(second_row[a], w[1]).astype(BF16)
        lrow[a * T : (a + 1) * T, T : 2 * T] = keep(row_pos >= 2, third) if a == 0 else third
    ys[T : 2 * T, :] = tmm(w[1], r1.astype(BF16)).astype(BF16)

    arrival.wait()
    for a in range(TR):
        rows = lrow[a * T : (a + 1) * T, :]
        obuf[a] = (samples[a].astype(F32) - mm(rows, ys[...])).astype(BF16)

    @pl.when(row_pos == 0)
    def _():
        obuf[0] = ys[0:T, :]

    @pl.when(row_pos == 1)
    def _():
        obuf[0] = ys[T : 2 * T, :]

    out = pltpu.make_async_copy(obuf, solved, sem)
    out.start()

    for a in range(TR):
        product = mmt(lrow[a * T : (a + 1) * T, :], lcol[...])
        for b in range(TC):
            rest = (m[b][a].astype(F32) - product[:, b * T : (b + 1) * T]).astype(BF16)
            rest = keep(place[3 + 2 * a + b] != 0, rest)
            slab[b, a] = lax.select(col_pos >= 2, rest, slab[0, 0]) if (a, b) == (0, 0) else rest

    @pl.when(col_pos == 0)
    def _():
        for a in range(1, TR):
            slab[0, a] = lrow[a * T : (a + 1) * T, 0:T]

        @pl.when(row_pos == 0)
        def _():
            slab[0, 0] = f0[0]

        @pl.when(row_pos >= 1)
        def _():
            slab[0, 0] = lrow[0:T, 0:T]

    @pl.when(col_pos == 1)
    def _():
        for a in range(1, TR):
            slab[0, a] = lrow[a * T : (a + 1) * T, T : 2 * T]

        @pl.when(row_pos >= 2)
        def _():
            slab[0, 0] = lrow[0:T, T : 2 * T]

    out.wait()


def finish_kernel(place, rows0, rows1, got, got_o, m0, m1, samples_far, *rest):
    *rest, samples, samples_sem = rest
    arrival = pltpu.make_async_copy(samples_far, samples, samples_sem)
    arrival.start()
    rest = (m0, m1, samples, *rest, arrival)

    @pl.when(place[2] == 0)
    def _():
        finish(0, place, rows0, rows1, got, got_o, *rest)

    @pl.when(place[2] == 1)
    def _():
        finish(1, place, rows0, rows1, got_o, got, *rest)


def body(front, fill, w, samples):
    x = lax.axis_index("x")
    z = lax.axis_index("z")
    y = lax.axis_index("y")
    k = lax.axis_index("core")
    tiles = front.transpose(2, 0, 1, 3) * fill.astype(BF16).transpose(2, 0, 1, 3)
    tiles = lax.optimization_barrier(tiles)

    panel = lax.optimization_barrier(tiles[0])

    piece = lax.dynamic_slice(samples, (0, 0, k * T), (1, T, T))
    send = jnp.concatenate([panel[0].reshape(Q, RB, T), piece.reshape(Q, RB, T)], axis=1)
    got = lax.all_to_all(send, ("x", "y"), 0, 0)

    right = lax.ppermute(panel, "y", [(0, 1)])
    left = lax.ppermute(panel, "y", [(0, 3)])
    far = lax.ppermute(right, "y", [(1, 2)])

    send = jnp.concatenate([got[0, :RB], got[Y, :RB], got[0, RB:]], axis=0)
    got = lax.all_to_all(jnp.broadcast_to(send[None], (Z,) + send.shape), "z", 0, 0)

    pairs = got.reshape(Y, 2, 3 * RB, T)[:, :, : 2 * RB, :].reshape(Y, 4 * RB, T)
    common = jnp.concatenate([got[1, :RB], got[0, 2 * RB :], got[1, 2 * RB :]], axis=0)
    send = jnp.concatenate([pairs, jnp.broadcast_to(common[None], (Y,) + common.shape)], axis=1)
    send = jnp.broadcast_to(send[None], (X,) + send.shape).reshape(Q, 7 * RB, T)
    got = lax.all_to_all(send, ("x", "y"), 0, 0)

    rest = tiles[1]
    place = jnp.stack([x * Z + z, y * K + k, k]).astype(jnp.int32)
    place = jnp.concatenate([place, fill.reshape(TR * TC)])

    own = lax.select(y == 0, panel, right + left + far)
    other = swap(own)
    rows0 = jnp.concatenate([lax.select(k == 0, own, other), w])
    rows1 = lax.select(k == 0, other, own)
    got_o = swap(got)

    vmem = pl.BlockSpec(memory_space=pltpu.VMEM)
    smem = pl.BlockSpec(memory_space=pltpu.SMEM)
    slab, solved = pl.pallas_call(
        finish_kernel,
        in_specs=[smem] + [vmem] * 6 + [pl.BlockSpec(memory_space=pltpu.HBM)],
        out_specs=[vmem, pl.BlockSpec(memory_space=pl.ANY)],
        out_shape=[
            jax.ShapeDtypeStruct((TC, TR, T, T), BF16),
            jax.ShapeDtypeStruct((TR, T, 2 * T), BF16),
        ],
        scratch_shapes=[
            pltpu.VMEM((TR * T, 2 * T), BF16),
            pltpu.VMEM((TC * T, 2 * T), BF16),
            pltpu.VMEM((2 * T, 2 * T), BF16),
            pltpu.VMEM((TR, T, 2 * T), BF16),
            pltpu.SemaphoreType.DMA,
            pltpu.VMEM((TR, T, 2 * T), BF16),
            pltpu.SemaphoreType.DMA,
        ],
        compiler_params=pltpu.CompilerParams(vmem_limit_bytes=20 * 1024 * 1024),
        name="finish",
    )(
        place,
        rows0,
        rows1,
        got,
        got_o,
        panel,
        rest,
        pltpu.with_memory_space_constraint(samples, pltpu.HBM),
    )
    return slab.transpose(1, 2, 0, 3), solved


def solution(mesh):
    fine = Mesh(mesh.devices.reshape(X, Z, Y, K), ("x", "z", "y", "core"))
    row, col = ("x", "z"), ("y", "core")
    in_specs = (P(None, row, None, col), P(None, row, None, col), P(), P(None, row))
    out_specs = (P(None, row, None, col), P(None, row))
    return jax.shard_map(body, mesh=fine, in_specs=in_specs, out_specs=out_specs, check_vma=False)
```

```python
import jax
import jax.numpy as jnp
from jax import lax
from jax.experimental import pallas as pl
from jax.experimental.pallas import tpu as pltpu
from jax.sharding import Mesh, PartitionSpec as P


X, Z, Y, K = 4, 8, 4, 2
T = 256
TR = 4
TC = 2
Q = X * Y
RB = T // Q
F32, BF16 = jnp.float32, jnp.bfloat16


def swap(v):
    return lax.ppermute(v, "core", [(0, 1), (1, 0)])


def mm(a, b):
    return lax.dot_general(a, b, (((1,), (0,)), ((), ())), preferred_element_type=F32)


def mmt(a, b):
    return lax.dot_general(a, b, (((1,), (1,)), ((), ())), preferred_element_type=F32)


def tmm(a, b):
    return lax.dot_general(a, b, (((0,), (0,)), ((), ())), preferred_element_type=F32)


def keep(cond, value):
    return jnp.where(cond, value, jnp.zeros_like(value))


def finish(k, place, f0, f1, g0, g1, m0, m1, samples, slab, solved, lrow, lcol, ys, obuf, sem, arrival):
    row_pos = place[0]
    col_pos = place[1]
    w = (f0[TR], f0[TR + 1])
    m = (m0, m1)

    def tile(ref, at):
        return ref[:, at * RB : (at + 1) * RB, :].reshape(T, T)

    def from_second(tile_second, first):
        return (tile_second.astype(F32) - mmt(first, l0_one)).astype(BF16)

    l0_one = mm(tile(g0, 4), w[0]).astype(BF16)
    first_col = [mm(tile(g0, 2 * k + b), w[0]).astype(BF16) for b in range(TC)]
    first_col[0] = keep(col_pos >= 1, first_col[0])
    y0 = tmm(w[0], jnp.concatenate([tile(g0, 5), tile(g1, 5)], axis=1)).astype(BF16)
    first_row = mm(f0[0:TR].reshape(TR * T, T), w[0]).astype(BF16)
    first_row = [first_row[a * T : (a + 1) * T] for a in range(TR)]
    first_row[0] = keep(row_pos >= 1, first_row[0])
    ys[0:T, :] = y0
    for b in range(TC):
        lcol[b * T : (b + 1) * T, 0:T] = first_col[b]
    for a in range(TR):
        lrow[a * T : (a + 1) * T, 0:T] = first_row[a]

    second_col = [from_second(tile(g1, 2 * k + b), first_col[b]) for b in range(TC)]
    second_row = [from_second(f1[a], first_row[a]) for a in range(TR)]
    r1 = jnp.concatenate([tile(g0, 6), tile(g1, 6)], axis=1).astype(F32) - mm(l0_one, y0)
    slab[0, 0] = second_row[0]
    for b in range(TC):
        third = mm(second_col[b], w[1]).astype(BF16)
        lcol[b * T : (b + 1) * T, T : 2 * T] = keep(col_pos >= 2, third) if b == 0 else third
    for a in range(TR):
        third = mm(second_row[a], w[1]).astype(BF16)
        lrow[a * T : (a + 1) * T, T : 2 * T] = keep(row_pos >= 2, third) if a == 0 else third
    ys[T : 2 * T, :] = tmm(w[1], r1.astype(BF16)).astype(BF16)

    arrival.wait()
    for a in range(TR):
        rows = lrow[a * T : (a + 1) * T, :]
        obuf[a] = (samples[a].astype(F32) - mm(rows, ys[...])).astype(BF16)

    @pl.when(row_pos == 0)
    def _():
        obuf[0] = ys[0:T, :]

    @pl.when(row_pos == 1)
    def _():
        obuf[0] = ys[T : 2 * T, :]

    out = pltpu.make_async_copy(obuf, solved, sem)
    out.start()

    for a in range(TR):
        product = mmt(lrow[a * T : (a + 1) * T, :], lcol[...])
        for b in range(TC):
            rest = (m[b][a].astype(F32) - product[:, b * T : (b + 1) * T]).astype(BF16)
            rest = keep(place[3 + 2 * a + b] != 0, rest)
            slab[b, a] = lax.select(col_pos >= 2, rest, slab[0, 0]) if (a, b) == (0, 0) else rest

    @pl.when(col_pos == 0)
    def _():
        for a in range(1, TR):
            slab[0, a] = lrow[a * T : (a + 1) * T, 0:T]

        @pl.when(row_pos == 0)
        def _():
            slab[0, 0] = f0[0]

        @pl.when(row_pos >= 1)
        def _():
            slab[0, 0] = lrow[0:T, 0:T]

    @pl.when(col_pos == 1)
    def _():
        for a in range(1, TR):
            slab[0, a] = lrow[a * T : (a + 1) * T, T : 2 * T]

        @pl.when(row_pos >= 2)
        def _():
            slab[0, 0] = lrow[0:T, T : 2 * T]

    out.wait()


def finish_kernel(place, rows0, rows1, got, got_o, m0, m1, samples_far, *rest):
    *rest, samples, samples_sem = rest
    arrival = pltpu.make_async_copy(samples_far, samples, samples_sem)
    arrival.start()
    rest = (m0, m1, samples, *rest, arrival)

    @pl.when(place[2] == 0)
    def _():
        finish(0, place, rows0, rows1, got, got_o, *rest)

    @pl.when(place[2] == 1)
    def _():
        finish(1, place, rows0, rows1, got_o, got, *rest)


def body(front, fill, w, samples):
    x = lax.axis_index("x")
    z = lax.axis_index("z")
    y = lax.axis_index("y")
    k = lax.axis_index("core")
    tiles = front.transpose(2, 0, 1, 3) * fill.astype(BF16).transpose(2, 0, 1, 3)
    tiles = lax.optimization_barrier(tiles)

    panel = lax.optimization_barrier(tiles[0])

    piece = lax.dynamic_slice(samples, (0, 0, k * T), (1, T, T))
    send = jnp.concatenate([panel[0].reshape(Q, RB, T), piece.reshape(Q, RB, T)], axis=1)
    got = lax.all_to_all(send, ("x", "y"), 0, 0)

    right = lax.ppermute(panel, "y", [(0, 1)])
    left = lax.ppermute(panel, "y", [(0, 3)])
    near = right + left
    far = lax.ppermute(near, ("y", "core"), [(2, 4), (7, 5)])

    send = jnp.concatenate([got[0, :RB], got[Y, :RB], got[0, RB:]], axis=0)
    got = lax.all_to_all(jnp.broadcast_to(send[None], (Z,) + send.shape), "z", 0, 0)

    pairs = got.reshape(Y, 2, 3 * RB, T)[:, :, : 2 * RB, :].reshape(Y, 4 * RB, T)
    common = jnp.concatenate([got[1, :RB], got[0, 2 * RB :], got[1, 2 * RB :]], axis=0)
    send = jnp.concatenate([pairs, jnp.broadcast_to(common[None], (Y,) + common.shape)], axis=1)
    send = jnp.broadcast_to(send[None], (X,) + send.shape).reshape(Q, 7 * RB, T)
    got = lax.all_to_all(send, ("x", "y"), 0, 0)

    rest = tiles[1]
    place = jnp.stack([x * Z + z, y * K + k, k]).astype(jnp.int32)
    place = jnp.concatenate([place, fill.reshape(TR * TC)])

    own = lax.select(y == 0, panel, near + far)
    other = swap(own)
    rows0 = jnp.concatenate([lax.select(k == 0, own, other), w])
    rows1 = lax.select(k == 0, other, own)
    got_o = swap(got)

    vmem = pl.BlockSpec(memory_space=pltpu.VMEM)
    smem = pl.BlockSpec(memory_space=pltpu.SMEM)
    slab, solved = pl.pallas_call(
        finish_kernel,
        in_specs=[smem] + [vmem] * 6 + [pl.BlockSpec(memory_space=pltpu.HBM)],
        out_specs=[vmem, pl.BlockSpec(memory_space=pl.ANY)],
        out_shape=[
            jax.ShapeDtypeStruct((TC, TR, T, T), BF16),
            jax.ShapeDtypeStruct((TR, T, 2 * T), BF16),
        ],
        scratch_shapes=[
            pltpu.VMEM((TR * T, 2 * T), BF16),
            pltpu.VMEM((TC * T, 2 * T), BF16),
            pltpu.VMEM((2 * T, 2 * T), BF16),
            pltpu.VMEM((TR, T, 2 * T), BF16),
            pltpu.SemaphoreType.DMA,
            pltpu.VMEM((TR, T, 2 * T), BF16),
            pltpu.SemaphoreType.DMA,
        ],
        compiler_params=pltpu.CompilerParams(vmem_limit_bytes=20 * 1024 * 1024),
        name="finish",
    )(
        place,
        rows0,
        rows1,
        got,
        got_o,
        panel,
        rest,
        pltpu.with_memory_space_constraint(samples, pltpu.HBM),
    )
    return slab.transpose(1, 2, 0, 3), solved


def solution(mesh):
    fine = Mesh(mesh.devices.reshape(X, Z, Y, K), ("x", "z", "y", "core"))
    row, col = ("x", "z"), ("y", "core")
    in_specs = (P(None, row, None, col), P(None, row, None, col), P(), P(None, row))
    out_specs = (P(None, row, None, col), P(None, row))
    return jax.shard_map(body, mesh=fine, in_specs=in_specs, out_specs=out_specs, check_vma=False)
```

```python
import jax
import jax.numpy as jnp
from jax import lax
from jax.experimental import pallas as pl
from jax.experimental.pallas import tpu as pltpu
from jax.sharding import Mesh, PartitionSpec as P


X, Z, Y, K = 4, 8, 4, 2
T = 256
TR = 4
TC = 2
Q = X * Y
RB = T // Q
F32, BF16 = jnp.float32, jnp.bfloat16


def swap(v):
    return lax.ppermute(v, "core", [(0, 1), (1, 0)])


def mm(a, b):
    return lax.dot_general(a, b, (((1,), (0,)), ((), ())), preferred_element_type=F32)


def mmt(a, b):
    return lax.dot_general(a, b, (((1,), (1,)), ((), ())), preferred_element_type=F32)


def tmm(a, b):
    return lax.dot_general(a, b, (((0,), (0,)), ((), ())), preferred_element_type=F32)


def keep(cond, value):
    return jnp.where(cond, value, jnp.zeros_like(value))


def finish(ends, place, f0, f1, g0, g1, m0, m1, samples, slab, solved, lrow, lcol, ys, obuf, sem, arrival):
    row_pos = place[0]
    col_pos = place[1]
    w = (f0[TR], f0[TR + 1])
    e0, e1 = ends
    m = (m0, m1)

    def tile(ref, at):
        return ref[:, at * RB : (at + 1) * RB, :].reshape(T, T)

    def from_second(tile_second, first):
        return (tile_second.astype(F32) - mmt(first, l0_one)).astype(BF16)

    l0_one = mm(tile(g0, e0), w[0]).astype(BF16)
    first_col = [mm(tile(g0, b), w[0]).astype(BF16) for b in range(TC)]
    first_col[0] = keep(col_pos >= 1, first_col[0])
    y0 = tmm(w[0], jnp.concatenate([tile(g0, e0 + 1), tile(g1, e1 + 1)], axis=1)).astype(BF16)
    first_row = mm(f0[0:TR].reshape(TR * T, T), w[0]).astype(BF16)
    first_row = [first_row[a * T : (a + 1) * T] for a in range(TR)]
    first_row[0] = keep(row_pos >= 1, first_row[0])
    ys[0:T, :] = y0
    for b in range(TC):
        lcol[b * T : (b + 1) * T, 0:T] = first_col[b]
    for a in range(TR):
        lrow[a * T : (a + 1) * T, 0:T] = first_row[a]

    second_col = [from_second(tile(g1, b), first_col[b]) for b in range(TC)]
    second_row = [from_second(f1[a], first_row[a]) for a in range(TR)]
    r1 = jnp.concatenate([tile(g0, e0 + 2), tile(g1, e1 + 2)], axis=1).astype(F32) - mm(l0_one, y0)
    slab[0, 0] = second_row[0]
    for b in range(TC):
        third = mm(second_col[b], w[1]).astype(BF16)
        lcol[b * T : (b + 1) * T, T : 2 * T] = keep(col_pos >= 2, third) if b == 0 else third
    for a in range(TR):
        third = mm(second_row[a], w[1]).astype(BF16)
        lrow[a * T : (a + 1) * T, T : 2 * T] = keep(row_pos >= 2, third) if a == 0 else third
    ys[T : 2 * T, :] = tmm(w[1], r1.astype(BF16)).astype(BF16)

    arrival.wait()
    for a in range(TR):
        rows = lrow[a * T : (a + 1) * T, :]
        obuf[a] = (samples[a].astype(F32) - mm(rows, ys[...])).astype(BF16)

    @pl.when(row_pos == 0)
    def _():
        obuf[0] = ys[0:T, :]

    @pl.when(row_pos == 1)
    def _():
        obuf[0] = ys[T : 2 * T, :]

    out = pltpu.make_async_copy(obuf, solved, sem)
    out.start()

    for a in range(TR):
        product = mmt(lrow[a * T : (a + 1) * T, :], lcol[...])
        for b in range(TC):
            rest = (m[b][a].astype(F32) - product[:, b * T : (b + 1) * T]).astype(BF16)
            rest = keep(place[3 + 2 * a + b] != 0, rest)
            slab[b, a] = lax.select(col_pos >= 2, rest, slab[0, 0]) if (a, b) == (0, 0) else rest

    @pl.when(col_pos == 0)
    def _():
        for a in range(1, TR):
            slab[0, a] = lrow[a * T : (a + 1) * T, 0:T]

        @pl.when(row_pos == 0)
        def _():
            slab[0, 0] = f0[0]

        @pl.when(row_pos >= 1)
        def _():
            slab[0, 0] = lrow[0:T, 0:T]

    @pl.when(col_pos == 1)
    def _():
        for a in range(1, TR):
            slab[0, a] = lrow[a * T : (a + 1) * T, T : 2 * T]

        @pl.when(row_pos >= 2)
        def _():
            slab[0, 0] = lrow[0:T, T : 2 * T]

    out.wait()


def finish_kernel(place, rows0, rows1, got, got_o, m0, m1, samples_far, *rest):
    *rest, samples, samples_sem = rest
    arrival = pltpu.make_async_copy(samples_far, samples, samples_sem)
    arrival.start()
    rest = (m0, m1, samples, *rest, arrival)

    @pl.when(place[2] == 0)
    def _():
        finish((4, 2), place, rows0, rows1, got, got_o, *rest)

    @pl.when(place[2] == 1)
    def _():
        finish((2, 4), place, rows0, rows1, got_o, got, *rest)


def body(front, fill, w, samples):
    x = lax.axis_index("x")
    z = lax.axis_index("z")
    y = lax.axis_index("y")
    k = lax.axis_index("core")
    piece = lax.dynamic_slice(samples, (0, 0, k * T), (1, T, T))
    piece, pattern = lax.optimization_barrier((piece, fill))
    tiles = front.transpose(2, 0, 1, 3) * pattern.astype(BF16).transpose(2, 0, 1, 3)
    tiles = lax.optimization_barrier(tiles)

    panel = lax.optimization_barrier(tiles[0])

    send = jnp.concatenate([panel[0].reshape(Q, RB, T), piece.reshape(Q, RB, T)], axis=1)
    got = lax.all_to_all(send, ("x", "y"), 0, 0)

    right = lax.ppermute(panel, "y", [(0, 1)])
    left = lax.ppermute(panel, "y", [(0, 3)])
    near = right + left
    far = lax.ppermute(near, ("y", "core"), [(2, 4), (7, 5)])

    send = jnp.concatenate([got[0, :RB], got[Y, :RB], got[0, RB:]], axis=0)
    got = lax.all_to_all(jnp.broadcast_to(send[None], (Z,) + send.shape), "z", 0, 0)

    pairs = got.reshape(Y, 2, 3 * RB, T)[:, :, : 2 * RB, :].reshape(Y, 4 * RB, T)
    common = jnp.concatenate([got[1, :RB], got[0, 2 * RB :], got[1, 2 * RB :]], axis=0)
    pairs = pairs.reshape(Y, 2, 2 * RB, T)
    pairs = lax.select(k == 0, pairs, pairs[:, ::-1]).reshape(Y, 4 * RB, T)
    send = jnp.concatenate([pairs, jnp.broadcast_to(common[None], (Y,) + common.shape)], axis=1)
    send = jnp.broadcast_to(send[None], (X,) + send.shape).reshape(Q, 7 * RB, T)
    got = lax.all_to_all(send, ("x", "y"), 0, 0)

    rest = tiles[1]
    place = jnp.stack([x * Z + z, y * K + k, k]).astype(jnp.int32)
    place = jnp.concatenate([place, fill.reshape(TR * TC)])

    own = lax.select(y == 0, panel, near + far)
    other = swap(own)
    rows0 = jnp.concatenate([lax.select(k == 0, own, other), w])
    rows1 = lax.select(k == 0, other, own)
    got_o = swap(got[:, 2 * RB :])

    vmem = pl.BlockSpec(memory_space=pltpu.VMEM)
    smem = pl.BlockSpec(memory_space=pltpu.SMEM)
    slab, solved = pl.pallas_call(
        finish_kernel,
        in_specs=[smem] + [vmem] * 6 + [pl.BlockSpec(memory_space=pltpu.HBM)],
        out_specs=[vmem, pl.BlockSpec(memory_space=pl.ANY)],
        out_shape=[
            jax.ShapeDtypeStruct((TC, TR, T, T), BF16),
            jax.ShapeDtypeStruct((TR, T, 2 * T), BF16),
        ],
        scratch_shapes=[
            pltpu.VMEM((TR * T, 2 * T), BF16),
            pltpu.VMEM((TC * T, 2 * T), BF16),
            pltpu.VMEM((2 * T, 2 * T), BF16),
            pltpu.VMEM((TR, T, 2 * T), BF16),
            pltpu.SemaphoreType.DMA,
            pltpu.VMEM((TR, T, 2 * T), BF16),
            pltpu.SemaphoreType.DMA,
        ],
        compiler_params=pltpu.CompilerParams(vmem_limit_bytes=20 * 1024 * 1024),
        name="finish",
    )(
        place,
        rows0,
        rows1,
        got,
        got_o,
        panel,
        rest,
        pltpu.with_memory_space_constraint(samples, pltpu.HBM),
    )
    return slab.transpose(1, 2, 0, 3), solved


def solution(mesh):
    fine = Mesh(mesh.devices.reshape(X, Z, Y, K), ("x", "z", "y", "core"))
    row, col = ("x", "z"), ("y", "core")
    in_specs = (P(None, row, None, col), P(None, row, None, col), P(), P(None, row))
    out_specs = (P(None, row, None, col), P(None, row))
    return jax.shard_map(body, mesh=fine, in_specs=in_specs, out_specs=out_specs, check_vma=False)
```

```python
import jax
import jax.numpy as jnp
from jax import lax
from jax.experimental import pallas as pl
from jax.experimental.pallas import tpu as pltpu
from jax.sharding import Mesh, PartitionSpec as P


X, Z, Y, K = 4, 8, 4, 2
T = 256
TR = 4
TC = 2
Q = X * Y
RB = T // Q
F32, BF16 = jnp.float32, jnp.bfloat16


def swap(v):
    return lax.ppermute(v, "core", [(0, 1), (1, 0)])


def mm(a, b):
    return lax.dot_general(a, b, (((1,), (0,)), ((), ())), preferred_element_type=F32)


def mmt(a, b):
    return lax.dot_general(a, b, (((1,), (1,)), ((), ())), preferred_element_type=F32)


def tmm(a, b):
    return lax.dot_general(a, b, (((0,), (0,)), ((), ())), preferred_element_type=F32)


def keep(cond, value):
    return jnp.where(cond, value, jnp.zeros_like(value))


def finish(ends, place, f0, f1, g0, g1, m0, m1, samples, slab, solved, lrow, lcol, ys, obuf, sem, arrival):
    row_pos = place[0]
    col_pos = place[1]
    w = (f0[TR], f0[TR + 1])
    e0, e1 = ends
    m = (m0, m1)

    def tile(ref, at):
        return ref[:, at * RB : (at + 1) * RB, :].reshape(T, T)

    def from_second(tile_second, first):
        return (tile_second.astype(F32) - mmt(first, l0_one)).astype(BF16)

    l0_one = mm(tile(g0, e0), w[0]).astype(BF16)
    first_col = [mm(tile(g0, b), w[0]).astype(BF16) for b in range(TC)]
    first_col[0] = keep(col_pos >= 1, first_col[0])
    y0 = tmm(w[0], jnp.concatenate([tile(g0, e0 + 1), tile(g1, e1 + 1)], axis=1)).astype(BF16)
    first_row = mm(f0[0:TR].reshape(TR * T, T), w[0]).astype(BF16)
    first_row = [first_row[a * T : (a + 1) * T] for a in range(TR)]
    first_row[0] = keep(row_pos >= 1, first_row[0])
    ys[0:T, :] = y0
    for b in range(TC):
        lcol[b * T : (b + 1) * T, 0:T] = first_col[b]
    for a in range(TR):
        lrow[a * T : (a + 1) * T, 0:T] = first_row[a]

    second_col = [from_second(tile(g1, b), first_col[b]) for b in range(TC)]
    second_row = [from_second(f1[a], first_row[a]) for a in range(TR)]
    r1 = jnp.concatenate([tile(g0, e0 + 2), tile(g1, e1 + 2)], axis=1).astype(F32) - mm(l0_one, y0)
    slab[0, 0] = second_row[0]
    for b in range(TC):
        third = mm(second_col[b], w[1]).astype(BF16)
        lcol[b * T : (b + 1) * T, T : 2 * T] = keep(col_pos >= 2, third) if b == 0 else third
    for a in range(TR):
        third = mm(second_row[a], w[1]).astype(BF16)
        lrow[a * T : (a + 1) * T, T : 2 * T] = keep(row_pos >= 2, third) if a == 0 else third
    ys[T : 2 * T, :] = tmm(w[1], r1.astype(BF16)).astype(BF16)

    arrival.wait()
    for a in range(TR):
        rows = lrow[a * T : (a + 1) * T, :]
        obuf[a] = (samples[a].astype(F32) - mm(rows, ys[...])).astype(BF16)

    @pl.when(row_pos == 0)
    def _():
        obuf[0] = ys[0:T, :]

    @pl.when(row_pos == 1)
    def _():
        obuf[0] = ys[T : 2 * T, :]

    out = pltpu.make_async_copy(obuf, solved, sem)
    out.start()

    for a in range(TR):
        product = mmt(lrow[a * T : (a + 1) * T, :], lcol[...])
        for b in range(TC):
            rest = (m[b][a].astype(F32) - product[:, b * T : (b + 1) * T]).astype(BF16)
            rest = keep(place[3 + 2 * a + b] != 0, rest)
            slab[b, a] = lax.select(col_pos >= 2, rest, slab[0, 0]) if (a, b) == (0, 0) else rest

    @pl.when(col_pos == 0)
    def _():
        for a in range(1, TR):
            slab[0, a] = lrow[a * T : (a + 1) * T, 0:T]

        @pl.when(row_pos == 0)
        def _():
            slab[0, 0] = f0[0]

        @pl.when(row_pos >= 1)
        def _():
            slab[0, 0] = lrow[0:T, 0:T]

    @pl.when(col_pos == 1)
    def _():
        for a in range(1, TR):
            slab[0, a] = lrow[a * T : (a + 1) * T, T : 2 * T]

        @pl.when(row_pos >= 2)
        def _():
            slab[0, 0] = lrow[0:T, T : 2 * T]

    out.wait()


def finish_kernel(place, rows0, rows1, got, got_o, m0, m1, samples_far, *rest):
    *rest, samples, samples_sem = rest
    arrival = pltpu.make_async_copy(samples_far, samples, samples_sem)
    arrival.start()
    rest = (m0, m1, samples, *rest, arrival)

    @pl.when(place[2] == 0)
    def _():
        finish((4, 2), place, rows0, rows1, got, got_o, *rest)

    @pl.when(place[2] == 1)
    def _():
        finish((2, 4), place, rows0, rows1, got_o, got, *rest)


def body(front, fill, w, samples):
    x = lax.axis_index("x")
    z = lax.axis_index("z")
    y = lax.axis_index("y")
    k = lax.axis_index("core")
    piece = lax.dynamic_slice(samples, (0, 0, k * T), (1, T, T))
    piece, pattern = lax.optimization_barrier((piece, fill))
    tiles = front.transpose(2, 0, 1, 3) * pattern.astype(BF16).transpose(2, 0, 1, 3)
    tiles = lax.optimization_barrier(tiles)

    panel = lax.optimization_barrier(tiles[0])

    send = jnp.concatenate([panel[0].reshape(Q, RB, T), piece.reshape(Q, RB, T)], axis=1)
    got = lax.all_to_all(send, ("x", "y"), 0, 0)

    near = lax.ppermute(panel, ("y", "core"), [(0, 2), (1, 7)])
    relay = lax.select(y == 0, panel, near)
    far = lax.ppermute(relay, ("y", "core"), [(2, 4), (7, 5), (0, 6), (1, 3)])

    send = jnp.concatenate([got[0, :RB], got[Y, :RB], got[0, RB:]], axis=0)
    got = lax.all_to_all(jnp.broadcast_to(send[None], (Z,) + send.shape), "z", 0, 0)

    pairs = got.reshape(Y, 2, 3 * RB, T)[:, :, : 2 * RB, :].reshape(Y, 4 * RB, T)
    common = jnp.concatenate([got[1, :RB], got[0, 2 * RB :], got[1, 2 * RB :]], axis=0)
    pairs = pairs.reshape(Y, 2, 2 * RB, T)
    pairs = lax.select(k == 0, pairs, pairs[:, ::-1]).reshape(Y, 4 * RB, T)
    send = jnp.concatenate([pairs, jnp.broadcast_to(common[None], (Y,) + common.shape)], axis=1)
    send = jnp.broadcast_to(send[None], (X,) + send.shape).reshape(Q, 7 * RB, T)
    got = lax.all_to_all(send, ("x", "y"), 0, 0)

    rest = tiles[1]
    place = jnp.stack([x * Z + z, y * K + k, k]).astype(jnp.int32)
    place = jnp.concatenate([place, fill.reshape(TR * TC)])

    own = lax.select(y == 0, panel, near + far)
    other = swap(own)
    rows0 = jnp.concatenate([lax.select(k == 0, own, other), w])
    rows1 = lax.select(k == 0, other, own)
    got_o = swap(got[:, 2 * RB :])

    vmem = pl.BlockSpec(memory_space=pltpu.VMEM)
    smem = pl.BlockSpec(memory_space=pltpu.SMEM)
    slab, solved = pl.pallas_call(
        finish_kernel,
        in_specs=[smem] + [vmem] * 6 + [pl.BlockSpec(memory_space=pltpu.HBM)],
        out_specs=[vmem, pl.BlockSpec(memory_space=pl.ANY)],
        out_shape=[
            jax.ShapeDtypeStruct((TC, TR, T, T), BF16),
            jax.ShapeDtypeStruct((TR, T, 2 * T), BF16),
        ],
        scratch_shapes=[
            pltpu.VMEM((TR * T, 2 * T), BF16),
            pltpu.VMEM((TC * T, 2 * T), BF16),
            pltpu.VMEM((2 * T, 2 * T), BF16),
            pltpu.VMEM((TR, T, 2 * T), BF16),
            pltpu.SemaphoreType.DMA,
            pltpu.VMEM((TR, T, 2 * T), BF16),
            pltpu.SemaphoreType.DMA,
        ],
        compiler_params=pltpu.CompilerParams(vmem_limit_bytes=20 * 1024 * 1024),
        name="finish",
    )(
        place,
        rows0,
        rows1,
        got,
        got_o,
        panel,
        rest,
        pltpu.with_memory_space_constraint(samples, pltpu.HBM),
    )
    return slab.transpose(1, 2, 0, 3), solved


def solution(mesh):
    fine = Mesh(mesh.devices.reshape(X, Z, Y, K), ("x", "z", "y", "core"))
    row, col = ("x", "z"), ("y", "core")
    in_specs = (P(None, row, None, col), P(None, row, None, col), P(), P(None, row))
    out_specs = (P(None, row, None, col), P(None, row))
    return jax.shard_map(body, mesh=fine, in_specs=in_specs, out_specs=out_specs, check_vma=False)
```

```python
import jax
import jax.numpy as jnp
from jax import lax
from jax.experimental import pallas as pl
from jax.experimental.pallas import tpu as pltpu
from jax.sharding import Mesh, PartitionSpec as P


X, Z, Y, K = 4, 8, 4, 2
T = 256
TR = 4
TC = 2
Q = X * Y
RB = T // Q
F32, BF16 = jnp.float32, jnp.bfloat16


def swap(v):
    return lax.ppermute(v, "core", [(0, 1), (1, 0)])


def mm(a, b):
    return lax.dot_general(a, b, (((1,), (0,)), ((), ())), preferred_element_type=F32)


def mmt(a, b):
    return lax.dot_general(a, b, (((1,), (1,)), ((), ())), preferred_element_type=F32)


def tmm(a, b):
    return lax.dot_general(a, b, (((0,), (0,)), ((), ())), preferred_element_type=F32)


def keep(cond, value):
    return jnp.where(cond, value, jnp.zeros_like(value))


def finish(ends, place, f0, f1, g0, g1, m0, m1, samples, slab, solved, lrow, lcol, ys, obuf, sem, arrival):
    row_pos = place[0]
    col_pos = place[1]
    w = (f0[TR], f0[TR + 1])
    e0, e1 = ends
    m = (m0, m1)

    def tile(ref, at):
        return ref[:, at * RB : (at + 1) * RB, :].reshape(T, T)

    def from_second(tile_second, first):
        return (tile_second.astype(F32) - mmt(first, l0_one)).astype(BF16)

    l0_one = mm(tile(g0, e0), w[0]).astype(BF16)
    first_col = [mm(tile(g0, b), w[0]).astype(BF16) for b in range(TC)]
    first_col[0] = keep(col_pos >= 1, first_col[0])
    y0 = tmm(w[0], jnp.concatenate([tile(g0, e0 + 1), tile(g1, e1 + 1)], axis=1)).astype(BF16)
    first_row = mm(f0[0:TR].reshape(TR * T, T), w[0]).astype(BF16)
    first_row = [first_row[a * T : (a + 1) * T] for a in range(TR)]
    first_row[0] = keep(row_pos >= 1, first_row[0])
    ys[0:T, :] = y0
    for b in range(TC):
        lcol[b * T : (b + 1) * T, 0:T] = first_col[b]
    for a in range(TR):
        lrow[a * T : (a + 1) * T, 0:T] = first_row[a]

    second_col = [from_second(tile(g1, b), first_col[b]) for b in range(TC)]
    second_row = [from_second(f1[a], first_row[a]) for a in range(TR)]
    r1 = jnp.concatenate([tile(g0, e0 + 2), tile(g1, e1 + 2)], axis=1).astype(F32) - mm(l0_one, y0)
    slab[0, 0] = second_row[0]
    for b in range(TC):
        third = mm(second_col[b], w[1]).astype(BF16)
        lcol[b * T : (b + 1) * T, T : 2 * T] = keep(col_pos >= 2, third) if b == 0 else third
    for a in range(TR):
        third = mm(second_row[a], w[1]).astype(BF16)
        lrow[a * T : (a + 1) * T, T : 2 * T] = keep(row_pos >= 2, third) if a == 0 else third
    ys[T : 2 * T, :] = tmm(w[1], r1.astype(BF16)).astype(BF16)

    arrival.wait()
    for a in range(TR):
        rows = lrow[a * T : (a + 1) * T, :]
        solved_tile = (samples[a].astype(F32) - mm(rows, ys[...])).astype(BF16)
        if a == 0:
            solved_tile = lax.select(row_pos == 0, ys[0:T, :], solved_tile)
            solved_tile = lax.select(row_pos == 1, ys[T : 2 * T, :], solved_tile)
        obuf[a] = solved_tile

    out = pltpu.make_async_copy(obuf, solved, sem)
    out.start()

    for a in range(TR):
        product = mmt(lrow[a * T : (a + 1) * T, :], lcol[...])
        for b in range(TC):
            rest = (m[b][a].astype(F32) - product[:, b * T : (b + 1) * T]).astype(BF16)
            rest = keep(place[3 + 2 * a + b] != 0, rest)
            slab[b, a] = lax.select(col_pos >= 2, rest, slab[0, 0]) if (a, b) == (0, 0) else rest

    @pl.when(col_pos == 0)
    def _():
        for a in range(1, TR):
            slab[0, a] = lrow[a * T : (a + 1) * T, 0:T]

        @pl.when(row_pos == 0)
        def _():
            slab[0, 0] = f0[0]

        @pl.when(row_pos >= 1)
        def _():
            slab[0, 0] = lrow[0:T, 0:T]

    @pl.when(col_pos == 1)
    def _():
        for a in range(1, TR):
            slab[0, a] = lrow[a * T : (a + 1) * T, T : 2 * T]

        @pl.when(row_pos >= 2)
        def _():
            slab[0, 0] = lrow[0:T, T : 2 * T]

    out.wait()


def finish_kernel(place, rows0, rows1, got, got_o, m0, m1, samples_far, *rest):
    *rest, samples, samples_sem = rest
    arrival = pltpu.make_async_copy(samples_far, samples, samples_sem)
    arrival.start()
    rest = (m0, m1, samples, *rest, arrival)

    @pl.when(place[2] == 0)
    def _():
        finish((4, 2), place, rows0, rows1, got, got_o, *rest)

    @pl.when(place[2] == 1)
    def _():
        finish((2, 4), place, rows0, rows1, got_o, got, *rest)


def body(front, fill, w, samples):
    x = lax.axis_index("x")
    z = lax.axis_index("z")
    y = lax.axis_index("y")
    k = lax.axis_index("core")
    piece = lax.dynamic_slice(samples, (0, 0, k * T), (1, T, T))
    piece, pattern = lax.optimization_barrier((piece, fill))
    tiles = front.transpose(2, 0, 1, 3) * pattern.astype(BF16).transpose(2, 0, 1, 3)
    tiles = lax.optimization_barrier(tiles)

    panel = lax.optimization_barrier(tiles[0])

    send = jnp.concatenate([panel[0].reshape(Q, RB, T), piece.reshape(Q, RB, T)], axis=1)
    got = lax.all_to_all(send, ("x", "y"), 0, 0)

    near = lax.ppermute(panel, ("y", "core"), [(0, 2), (1, 7)])
    relay = lax.select(y == 0, panel, near)
    far = lax.ppermute(relay, ("y", "core"), [(2, 4), (7, 5), (0, 6), (1, 3)])

    send = jnp.concatenate([got[0, :RB], got[Y, :RB], got[0, RB:]], axis=0)
    got = lax.all_to_all(jnp.broadcast_to(send[None], (Z,) + send.shape), "z", 0, 0)

    pairs = got.reshape(Y, 2, 3 * RB, T)[:, :, : 2 * RB, :].reshape(Y, 4 * RB, T)
    common = jnp.concatenate([got[1, :RB], got[0, 2 * RB :], got[1, 2 * RB :]], axis=0)
    pairs = pairs.reshape(Y, 2, 2 * RB, T)
    pairs = lax.select(k == 0, pairs, pairs[:, ::-1]).reshape(Y, 4 * RB, T)
    send = jnp.concatenate([pairs, jnp.broadcast_to(common[None], (Y,) + common.shape)], axis=1)
    send = jnp.broadcast_to(send[None], (X,) + send.shape).reshape(Q, 7 * RB, T)
    got = lax.all_to_all(send, ("x", "y"), 0, 0)

    rest = tiles[1]
    place = jnp.stack([x * Z + z, y * K + k, k]).astype(jnp.int32)
    place = jnp.concatenate([place, fill.reshape(TR * TC)])

    own = lax.select(y == 0, panel, near + far)
    other = swap(own)
    rows0 = jnp.concatenate([lax.select(k == 0, own, other), w])
    rows1 = lax.select(k == 0, other, own)
    got_o = swap(got[:, 2 * RB :])

    vmem = pl.BlockSpec(memory_space=pltpu.VMEM)
    smem = pl.BlockSpec(memory_space=pltpu.SMEM)
    slab, solved = pl.pallas_call(
        finish_kernel,
        in_specs=[smem] + [vmem] * 6 + [pl.BlockSpec(memory_space=pltpu.HBM)],
        out_specs=[vmem, pl.BlockSpec(memory_space=pl.ANY)],
        out_shape=[
            jax.ShapeDtypeStruct((TC, TR, T, T), BF16),
            jax.ShapeDtypeStruct((TR, T, 2 * T), BF16),
        ],
        scratch_shapes=[
            pltpu.VMEM((TR * T, 2 * T), BF16),
            pltpu.VMEM((TC * T, 2 * T), BF16),
            pltpu.VMEM((2 * T, 2 * T), BF16),
            pltpu.VMEM((TR, T, 2 * T), BF16),
            pltpu.SemaphoreType.DMA,
            pltpu.VMEM((TR, T, 2 * T), BF16),
            pltpu.SemaphoreType.DMA,
        ],
        compiler_params=pltpu.CompilerParams(vmem_limit_bytes=20 * 1024 * 1024),
        name="finish",
    )(
        place,
        rows0,
        rows1,
        got,
        got_o,
        panel,
        rest,
        pltpu.with_memory_space_constraint(samples, pltpu.HBM),
    )
    return slab.transpose(1, 2, 0, 3), solved


def solution(mesh):
    fine = Mesh(mesh.devices.reshape(X, Z, Y, K), ("x", "z", "y", "core"))
    row, col = ("x", "z"), ("y", "core")
    in_specs = (P(None, row, None, col), P(None, row, None, col), P(), P(None, row))
    out_specs = (P(None, row, None, col), P(None, row))
    return jax.shard_map(body, mesh=fine, in_specs=in_specs, out_specs=out_specs, check_vma=False)
```

```python
import jax
import jax.numpy as jnp
from jax import lax
from jax.experimental import pallas as pl
from jax.experimental.pallas import tpu as pltpu
from jax.sharding import Mesh, PartitionSpec as P


X, Z, Y, K = 4, 8, 4, 2
T = 256
TR = 4
TC = 2
Q = X * Y
RB = T // Q
F32, BF16 = jnp.float32, jnp.bfloat16


def swap(v):
    return lax.ppermute(v, "core", [(0, 1), (1, 0)])


def mm(a, b):
    return lax.dot_general(a, b, (((1,), (0,)), ((), ())), preferred_element_type=F32)


def mmt(a, b):
    return lax.dot_general(a, b, (((1,), (1,)), ((), ())), preferred_element_type=F32)


def tmm(a, b):
    return lax.dot_general(a, b, (((0,), (0,)), ((), ())), preferred_element_type=F32)


def keep(cond, value):
    return jnp.where(cond, value, jnp.zeros_like(value))


def finish(ends, place, f0, lrow, lead, g0, g1, m0, m1, samples, slab, solved, lcol, ys, obuf, sem, arrival):
    row_pos = place[0]
    col_pos = place[1]
    w = (f0[TR], f0[TR + 1])
    e0, e1 = ends
    m = (m0, m1)

    def tile(ref, at):
        return ref[:, at * RB : (at + 1) * RB, :].reshape(T, T)

    def from_second(tile_second, first):
        return (tile_second.astype(F32) - mmt(first, l0_one)).astype(BF16)

    l0_one = lead[0]
    slab[0, 0] = lead[1]
    first_col = [mm(tile(g0, b), w[0]).astype(BF16) for b in range(TC)]
    first_col[0] = keep(col_pos >= 1, first_col[0])
    y0 = tmm(w[0], jnp.concatenate([tile(g0, e0), tile(g1, e1)], axis=1)).astype(BF16)
    ys[0:T, :] = y0
    for b in range(TC):
        lcol[b * T : (b + 1) * T, 0:T] = first_col[b]
    r1 = jnp.concatenate([tile(g0, e0 + 1), tile(g1, e1 + 1)], axis=1).astype(F32) - mm(l0_one, y0)
    second_col = [from_second(tile(g1, b), first_col[b]) for b in range(TC)]
    ys[T : 2 * T, :] = tmm(w[1], r1.astype(BF16)).astype(BF16)
    for b in range(TC):
        third = mm(second_col[b], w[1]).astype(BF16)
        lcol[b * T : (b + 1) * T, T : 2 * T] = keep(col_pos >= 2, third) if b == 0 else third

    arrival.wait()
    for a in range(TR):
        rows = lrow[a * T : (a + 1) * T, :]
        solved_tile = (samples[a].astype(F32) - mm(rows, ys[...])).astype(BF16)
        if a == 0:
            solved_tile = lax.select(row_pos == 0, ys[0:T, :], solved_tile)
            solved_tile = lax.select(row_pos == 1, ys[T : 2 * T, :], solved_tile)
        obuf[a] = solved_tile

    out = pltpu.make_async_copy(obuf, solved, sem)
    out.start()

    for a in range(TR):
        product = mmt(lrow[a * T : (a + 1) * T, :], lcol[...])
        for b in range(TC):
            rest = (m[b][a].astype(F32) - product[:, b * T : (b + 1) * T]).astype(BF16)
            rest = keep(place[3 + 2 * a + b] != 0, rest)
            slab[b, a] = lax.select(col_pos >= 2, rest, slab[0, 0]) if (a, b) == (0, 0) else rest

    @pl.when(col_pos == 0)
    def _():
        for a in range(1, TR):
            slab[0, a] = lrow[a * T : (a + 1) * T, 0:T]

        @pl.when(row_pos == 0)
        def _():
            slab[0, 0] = f0[0]

        @pl.when(row_pos >= 1)
        def _():
            slab[0, 0] = lrow[0:T, 0:T]

    @pl.when(col_pos == 1)
    def _():
        for a in range(1, TR):
            slab[0, a] = lrow[a * T : (a + 1) * T, T : 2 * T]

        @pl.when(row_pos >= 2)
        def _():
            slab[0, 0] = lrow[0:T, T : 2 * T]

    out.wait()


def head_kernel(place, rows0, rows1, one, lrow, lead):
    row_pos = place[0]
    w = (rows0[TR], rows0[TR + 1])
    l0_one = mm(one[...], w[0]).astype(BF16)
    lead[0] = l0_one
    first = mm(rows0[0:TR].reshape(TR * T, T), w[0]).astype(BF16)
    for a in range(TR):
        rows = slice(a * T, (a + 1) * T)
        left = keep(row_pos >= 1, first[rows]) if a == 0 else first[rows]
        second = (rows1[a].astype(F32) - mmt(left, l0_one)).astype(BF16)
        third = mm(second, w[1]).astype(BF16)
        if a == 0:
            lead[1] = second
            third = keep(row_pos >= 2, third)
        lrow[rows, 0:T] = left
        lrow[rows, T : 2 * T] = third


def finish_kernel(place, rows0, lrow, lead, got, got_o, m0, m1, samples_far, *rest):
    *rest, samples, samples_sem = rest
    arrival = pltpu.make_async_copy(samples_far, samples, samples_sem)
    arrival.start()
    rest = (m0, m1, samples, *rest, arrival)

    @pl.when(place[2] == 0)
    def _():
        finish((5, 2), place, rows0, lrow, lead, got, got_o, *rest)

    @pl.when(place[2] == 1)
    def _():
        finish((2, 5), place, rows0, lrow, lead, got_o, got, *rest)


def body(front, fill, w, samples):
    x = lax.axis_index("x")
    z = lax.axis_index("z")
    y = lax.axis_index("y")
    k = lax.axis_index("core")
    piece = lax.dynamic_slice(samples, (0, 0, k * T), (1, T, T))
    piece, pattern = lax.optimization_barrier((piece, fill))
    tiles = front.transpose(2, 0, 1, 3) * pattern.astype(BF16).transpose(2, 0, 1, 3)
    tiles = lax.optimization_barrier(tiles)

    panel = lax.optimization_barrier(tiles[0])

    send = jnp.concatenate([panel[0].reshape(Q, RB, T), piece.reshape(Q, RB, T)], axis=1)
    got = lax.all_to_all(send, ("x", "y"), 0, 0)

    near = lax.ppermute(panel, ("y", "core"), [(0, 2), (1, 7)])
    relay = lax.select(y == 0, panel, near)
    far = lax.ppermute(relay, ("y", "core"), [(2, 4), (7, 5), (0, 6), (1, 3)])

    send = jnp.concatenate([got[0, :RB], got[Y, :RB], got[0, RB:]], axis=0)
    got = lax.all_to_all(jnp.broadcast_to(send[None], (Z,) + send.shape), "z", 0, 0)

    pairs = got.reshape(Y, 2, 3 * RB, T)[:, :, : 2 * RB, :].reshape(Y, 4 * RB, T)
    tile_one = jnp.broadcast_to(got[1:2, :RB], (Y, RB, T))
    samp = jnp.concatenate([got[0, 2 * RB :], got[1, 2 * RB :]], axis=0)
    samp = jnp.broadcast_to(samp[None], (Y,) + samp.shape)
    pairs = pairs.reshape(Y, 2, 2 * RB, T)
    pairs = lax.select(k == 0, pairs, pairs[:, ::-1])
    send = jnp.concatenate([pairs[:, 0], tile_one, pairs[:, 1], samp], axis=1)
    send = jnp.broadcast_to(send[None], (X,) + send.shape).reshape(Q, 7 * RB, T)
    got = lax.all_to_all(send, ("x", "y"), 0, 0)

    rest = tiles[1]
    place = jnp.stack([x * Z + z, y * K + k, k]).astype(jnp.int32)
    place = jnp.concatenate([place, fill.reshape(TR * TC)])

    own = lax.select(y == 0, panel, near + far)
    other = swap(own)
    rows0 = jnp.concatenate([lax.select(k == 0, own, other), w])
    rows1 = lax.select(k == 0, other, own)
    one = got[:, 2 * RB : 3 * RB]
    one = lax.select(k == 0, one, swap(one)).reshape(T, T)
    got_o = swap(got[:, 3 * RB :])

    vmem = pl.BlockSpec(memory_space=pltpu.VMEM)
    smem = pl.BlockSpec(memory_space=pltpu.SMEM)
    lrow, lead = pl.pallas_call(
        head_kernel,
        in_specs=[smem] + [vmem] * 3,
        out_specs=[vmem, vmem],
        out_shape=[
            jax.ShapeDtypeStruct((TR * T, 2 * T), BF16),
            jax.ShapeDtypeStruct((2, T, T), BF16),
        ],
        compiler_params=pltpu.CompilerParams(vmem_limit_bytes=16 * 1024 * 1024),
        name="head",
    )(place, rows0, rows1, one)
    slab, solved = pl.pallas_call(
        finish_kernel,
        in_specs=[smem] + [vmem] * 7 + [pl.BlockSpec(memory_space=pltpu.HBM)],
        out_specs=[vmem, pl.BlockSpec(memory_space=pl.ANY)],
        out_shape=[
            jax.ShapeDtypeStruct((TC, TR, T, T), BF16),
            jax.ShapeDtypeStruct((TR, T, 2 * T), BF16),
        ],
        scratch_shapes=[
            pltpu.VMEM((TC * T, 2 * T), BF16),
            pltpu.VMEM((2 * T, 2 * T), BF16),
            pltpu.VMEM((TR, T, 2 * T), BF16),
            pltpu.SemaphoreType.DMA,
            pltpu.VMEM((TR, T, 2 * T), BF16),
            pltpu.SemaphoreType.DMA,
        ],
        compiler_params=pltpu.CompilerParams(vmem_limit_bytes=20 * 1024 * 1024),
        name="finish",
    )(
        place,
        rows0,
        lrow,
        lead,
        got,
        got_o,
        panel,
        rest,
        pltpu.with_memory_space_constraint(samples, pltpu.HBM),
    )
    return slab.transpose(1, 2, 0, 3), solved


def solution(mesh):
    fine = Mesh(mesh.devices.reshape(X, Z, Y, K), ("x", "z", "y", "core"))
    row, col = ("x", "z"), ("y", "core")
    in_specs = (P(None, row, None, col), P(None, row, None, col), P(), P(None, row))
    out_specs = (P(None, row, None, col), P(None, row))
    return jax.shard_map(body, mesh=fine, in_specs=in_specs, out_specs=out_specs, check_vma=False)
```

```python
import jax
import jax.numpy as jnp
from jax import lax
from jax.experimental import pallas as pl
from jax.experimental.pallas import tpu as pltpu
from jax.sharding import Mesh, PartitionSpec as P


X, Z, Y, K = 4, 8, 4, 2
T = 256
TR = 4
TC = 2
Q = X * Y
RB = T // Q
F32, BF16 = jnp.float32, jnp.bfloat16


def swap(v):
    return lax.ppermute(v, "core", [(0, 1), (1, 0)])


def mm(a, b):
    return lax.dot_general(a, b, (((1,), (0,)), ((), ())), preferred_element_type=F32)


def mmt(a, b):
    return lax.dot_general(a, b, (((1,), (1,)), ((), ())), preferred_element_type=F32)


def tmm(a, b):
    return lax.dot_general(a, b, (((0,), (0,)), ((), ())), preferred_element_type=F32)


def keep(cond, value):
    return jnp.where(cond, value, jnp.zeros_like(value))


def finish(ends, place, f0, lrow, lead, g0, g1, m0, m1, samples, slab, solved, lcol, ys, obuf, sem):
    row_pos = place[0]
    col_pos = place[1]
    w = (f0[TR], f0[TR + 1])
    e0, e1 = ends
    m = (m0, m1)

    def tile(ref, at):
        return ref[:, at * RB : (at + 1) * RB, :].reshape(T, T)

    def from_second(tile_second, first):
        return (tile_second.astype(F32) - mmt(first, l0_one)).astype(BF16)

    l0_one = lead[0]
    slab[0, 0] = lead[1]
    first_col = [mm(tile(g0, b), w[0]).astype(BF16) for b in range(TC)]
    first_col[0] = keep(col_pos >= 1, first_col[0])
    y0 = tmm(w[0], jnp.concatenate([tile(g0, e0), tile(g1, e1)], axis=1)).astype(BF16)
    ys[0:T, :] = y0
    for b in range(TC):
        lcol[b * T : (b + 1) * T, 0:T] = first_col[b]
    r1 = jnp.concatenate([tile(g0, e0 + 1), tile(g1, e1 + 1)], axis=1).astype(F32) - mm(l0_one, y0)
    second_col = [from_second(tile(g1, b), first_col[b]) for b in range(TC)]
    ys[T : 2 * T, :] = tmm(w[1], r1.astype(BF16)).astype(BF16)
    for b in range(TC):
        third = mm(second_col[b], w[1]).astype(BF16)
        lcol[b * T : (b + 1) * T, T : 2 * T] = keep(col_pos >= 2, third) if b == 0 else third

    for a in range(TR):
        rows = lrow[a * T : (a + 1) * T, :]
        solved_tile = (samples[a].astype(F32) - mm(rows, ys[...])).astype(BF16)
        if a == 0:
            solved_tile = lax.select(row_pos == 0, ys[0:T, :], solved_tile)
            solved_tile = lax.select(row_pos == 1, ys[T : 2 * T, :], solved_tile)
        obuf[a] = solved_tile

    out = pltpu.make_async_copy(obuf, solved, sem)
    out.start()

    for a in range(TR):
        product = mmt(lrow[a * T : (a + 1) * T, :], lcol[...])
        for b in range(TC):
            rest = (m[b][a].astype(F32) - product[:, b * T : (b + 1) * T]).astype(BF16)
            rest = keep(place[3 + 2 * a + b] != 0, rest)
            slab[b, a] = lax.select(col_pos >= 2, rest, slab[0, 0]) if (a, b) == (0, 0) else rest

    @pl.when(col_pos == 0)
    def _():
        for a in range(1, TR):
            slab[0, a] = lrow[a * T : (a + 1) * T, 0:T]

        @pl.when(row_pos == 0)
        def _():
            slab[0, 0] = f0[0]

        @pl.when(row_pos >= 1)
        def _():
            slab[0, 0] = lrow[0:T, 0:T]

    @pl.when(col_pos == 1)
    def _():
        for a in range(1, TR):
            slab[0, a] = lrow[a * T : (a + 1) * T, T : 2 * T]

        @pl.when(row_pos >= 2)
        def _():
            slab[0, 0] = lrow[0:T, T : 2 * T]

    out.wait()


def head_kernel(place, rows0, rows1, one, samples_far, lrow, lead, samples, sem):
    arrival = pltpu.make_async_copy(samples_far, samples, sem)
    arrival.start()
    row_pos = place[0]
    w = (rows0[TR], rows0[TR + 1])
    l0_one = mm(one[...], w[0]).astype(BF16)
    lead[0] = l0_one
    first = mm(rows0[0:TR].reshape(TR * T, T), w[0]).astype(BF16)
    for a in range(TR):
        rows = slice(a * T, (a + 1) * T)
        left = keep(row_pos >= 1, first[rows]) if a == 0 else first[rows]
        second = (rows1[a].astype(F32) - mmt(left, l0_one)).astype(BF16)
        third = mm(second, w[1]).astype(BF16)
        if a == 0:
            lead[1] = second
            third = keep(row_pos >= 2, third)
        lrow[rows, 0:T] = left
        lrow[rows, T : 2 * T] = third
    arrival.wait()


def finish_kernel(place, rows0, lrow, lead, got, got_o, *rest):
    @pl.when(place[2] == 0)
    def _():
        finish((5, 2), place, rows0, lrow, lead, got, got_o, *rest)

    @pl.when(place[2] == 1)
    def _():
        finish((2, 5), place, rows0, lrow, lead, got_o, got, *rest)


def body(front, fill, w, samples):
    x = lax.axis_index("x")
    z = lax.axis_index("z")
    y = lax.axis_index("y")
    k = lax.axis_index("core")
    piece = lax.dynamic_slice(samples, (0, 0, k * T), (1, T, T))
    piece, pattern = lax.optimization_barrier((piece, fill))
    tiles = front.transpose(2, 0, 1, 3) * pattern.astype(BF16).transpose(2, 0, 1, 3)
    tiles = lax.optimization_barrier(tiles)

    panel = lax.optimization_barrier(tiles[0])

    send = jnp.concatenate([panel[0].reshape(Q, RB, T), piece.reshape(Q, RB, T)], axis=1)
    got = lax.all_to_all(send, ("x", "y"), 0, 0)

    near = lax.ppermute(panel, ("y", "core"), [(0, 2), (1, 7)])
    relay = lax.select(y == 0, panel, near)
    far = lax.ppermute(relay, ("y", "core"), [(2, 4), (7, 5), (0, 6), (1, 3)])

    send = jnp.concatenate([got[0, :RB], got[Y, :RB], got[0, RB:]], axis=0)
    got = lax.all_to_all(jnp.broadcast_to(send[None], (Z,) + send.shape), "z", 0, 0)

    pairs = got.reshape(Y, 2, 3 * RB, T)[:, :, : 2 * RB, :].reshape(Y, 4 * RB, T)
    tile_one = jnp.broadcast_to(got[1:2, :RB], (Y, RB, T))
    samp = jnp.concatenate([got[0, 2 * RB :], got[1, 2 * RB :]], axis=0)
    samp = jnp.broadcast_to(samp[None], (Y,) + samp.shape)
    pairs = pairs.reshape(Y, 2, 2 * RB, T)
    pairs = lax.select(k == 0, pairs, pairs[:, ::-1])
    send = jnp.concatenate([pairs[:, 0], tile_one, pairs[:, 1], samp], axis=1)
    send = jnp.broadcast_to(send[None], (X,) + send.shape).reshape(Q, 7 * RB, T)
    got = lax.all_to_all(send, ("x", "y"), 0, 0)

    rest = tiles[1]
    place = jnp.stack([x * Z + z, y * K + k, k]).astype(jnp.int32)
    place = jnp.concatenate([place, fill.reshape(TR * TC)])

    own = lax.select(y == 0, panel, near + far)
    other = swap(own)
    rows0 = jnp.concatenate([lax.select(k == 0, own, other), w])
    rows1 = lax.select(k == 0, other, own)
    one = got[:, 2 * RB : 3 * RB]
    one = lax.select(k == 0, one, swap(one)).reshape(T, T)
    got_o = swap(got[:, 3 * RB :])

    vmem = pl.BlockSpec(memory_space=pltpu.VMEM)
    smem = pl.BlockSpec(memory_space=pltpu.SMEM)
    lrow, lead, samples_near = pl.pallas_call(
        head_kernel,
        in_specs=[smem] + [vmem] * 3 + [pl.BlockSpec(memory_space=pltpu.HBM)],
        out_specs=[vmem, vmem, vmem],
        out_shape=[
            jax.ShapeDtypeStruct((TR * T, 2 * T), BF16),
            jax.ShapeDtypeStruct((2, T, T), BF16),
            jax.ShapeDtypeStruct((TR, T, 2 * T), BF16),
        ],
        scratch_shapes=[pltpu.SemaphoreType.DMA],
        compiler_params=pltpu.CompilerParams(vmem_limit_bytes=16 * 1024 * 1024),
        name="head",
    )(place, rows0, rows1, one, pltpu.with_memory_space_constraint(samples, pltpu.HBM))
    slab, solved = pl.pallas_call(
        finish_kernel,
        in_specs=[smem] + [vmem] * 8,
        out_specs=[vmem, pl.BlockSpec(memory_space=pl.ANY)],
        out_shape=[
            jax.ShapeDtypeStruct((TC, TR, T, T), BF16),
            jax.ShapeDtypeStruct((TR, T, 2 * T), BF16),
        ],
        scratch_shapes=[
            pltpu.VMEM((TC * T, 2 * T), BF16),
            pltpu.VMEM((2 * T, 2 * T), BF16),
            pltpu.VMEM((TR, T, 2 * T), BF16),
            pltpu.SemaphoreType.DMA,
        ],
        compiler_params=pltpu.CompilerParams(vmem_limit_bytes=20 * 1024 * 1024),
        name="finish",
    )(
        place,
        rows0,
        lrow,
        lead,
        got,
        got_o,
        panel,
        rest,
        samples_near,
    )
    return slab.transpose(1, 2, 0, 3), solved


def solution(mesh):
    fine = Mesh(mesh.devices.reshape(X, Z, Y, K), ("x", "z", "y", "core"))
    row, col = ("x", "z"), ("y", "core")
    in_specs = (P(None, row, None, col), P(None, row, None, col), P(), P(None, row))
    out_specs = (P(None, row, None, col), P(None, row))
    return jax.shard_map(body, mesh=fine, in_specs=in_specs, out_specs=out_specs, check_vma=False)
```
